768 devices in a mesh: dig: 96 (over x, z, core), cross: 8 (over y).
Axes of the slice: x: 4, y: 8, z: 12, core: 2. Of those that a mesh axis runs over, the one named last changes fastest.
Arguments:
- rhs_force: float32 [3, 384, 64, 256], P(None, 'dig', 'cross'), may hold values from -24 to 24
- moduli: float32 [384, 64, 256], P('dig', 'cross'), may hold values from 0.5 to 8
- fixed_nodes: int32 [384, 64, 256], P('dig', 'cross'), may hold values 0 or 1
- contact_nodes: int32 [384, 64, 256], P('dig', 'cross'), may hold values 0 or 1
Outputs:
- solution: float32 [3, 384, 64, 256], P(None, 'dig', 'cross')
- residual: float32 [3, 384, 64, 256], P(None, 'dig', 'cross')
The draws below stay inside these ranges and needn't reach their ends.
All inputs are finite; a program needn't handle non-finite values. No bound on the sum of `fixed_nodes` or of `contact_nodes` on one device may be relied on, other than what follows from the above.
Results may differ from the reference program's by a relative error of at most 0.039.
Values sent between devices are 32-bit elements; how exact they have to be, the bound alone decides.
No kernel may reach another device: no remote copies, remote signals or barrier semaphores. Data moves between devices by JAX's collectives and lax.ppermute only.
A program may use at most 32 MiB of HBM per device.

```python
import math
import jax
import jax.numpy as jnp
import numpy as np
from jax import lax

ITERS = 3
NX = 384
NY = 64
NZ = 256


def place_ends(values, rng, least, high):
    longest = values.shape.index(max(values.shape))
    spots = []
    for shift in (0, 1):
        where = [jax.random.randint(jax.random.fold_in(rng, axis), (), 0, length) for axis, length in enumerate(values.shape)]
        where[longest] = (where[longest] + shift) % values.shape[longest]
        spots.append(tuple(where))
    return values.at[spots[0]].set(least).at[spots[1]].set(high)


def levels(key, shape, shards, smallest, top_value):
    def one(axis_at, blocks):
        steps = jax.random.uniform(jax.random.fold_in(jax.random.fold_in(key, 6), axis_at), (blocks,), jnp.float32, smallest / len(shards), top_value / len(shards))
        return jnp.repeat(jnp.exp(steps), shape[axis_at] // blocks).reshape((-1,) + (1,) * (len(shape) - axis_at - 1))

    level = one(*shards[0])
    for cut in shards[1:]:
        level = level * one(*cut)
    return level


def normal_values(key, extent, scale, bound, cuts=(), held_as=jnp.bfloat16):
    values = scale * jax.random.normal(key, extent, jnp.float32)
    if cuts:
        values = values * levels(key, extent, cuts, -0.22, 0.18)
    return jnp.clip(values, -bound, bound).astype(held_as)


def setup_inputs(seed: int = 0) -> dict:
    key_list = jax.random.split(jax.random.key(seed), 5)
    return {
        "rhs_force": normal_values(key_list[0], (3, NX, NY, NZ), 4.0, 24.0, ((1, 96), (2, 8)), jnp.float32),
        "moduli": jnp.clip(jnp.exp(math.log(8.0) - 2.7725887 * jax.random.uniform(key_list[1], (NX, NY, NZ), jnp.float32) ** levels(key_list[1], (NX, NY, NZ), ((0, 96), (1, 8)), -0.2, 0.2)), 0.5, 8.0),
        "fixed_nodes": place_ends((jax.random.randint(key_list[2], (NX, NY, NZ), 0, 16) < 1).astype(jnp.int32), jax.random.fold_in(key_list[2], 1), 0, 1),
        "contact_nodes": place_ends((jax.random.randint(key_list[3], (NX, NY, NZ), 0, 4) < 1).astype(jnp.int32), jax.random.fold_in(key_list[3], 1), 0, 1),
    }


POISSON = 0.3
PENALTY = 6.0
CORNER_LIST = ((0, 0, 0), (0, 0, 1), (0, 1, 0), (0, 1, 1), (1, 0, 0), (1, 0, 1), (1, 1, 0), (1, 1, 1))

def element_matrix():
    lame_first = POISSON / ((1.0 + POISSON) * (1.0 - 2.0 * POISSON))
    shear = 0.5 / (1.0 + POISSON)
    elastic = np.zeros((6, 6))
    elastic[:3, :3] = lame_first
    for dim_one in range(3):
        elastic[dim_one, dim_one] += 2.0 * shear
        elastic[dim_one + 3, dim_one + 3] = shear
    points = (0.5 - 0.5 / math.sqrt(3.0), 0.5 + 0.5 / math.sqrt(3.0))
    matrix = np.zeros((24, 24))
    for point_x in points:
        for point_y in points:
            for point_z in points:
                coords = (point_x, point_y, point_z)
                strain = np.zeros((6, 24))
                for corner_id in range(8):
                    corner = CORNER_LIST[corner_id]
                    grads = []
                    for dim_one in range(3):
                        product = 1.0
                        for dim_two in range(3):
                            if dim_two == dim_one:
                                factor = 1.0 if corner[dim_two] else -1.0
                            else:
                                factor = coords[dim_two] if corner[dim_two] else 1.0 - coords[dim_two]
                            product = product * factor
                        grads.append(product)
                    for dim_one in range(3):
                        strain[dim_one, dim_one * 8 + corner_id] = grads[dim_one]
                    strain[3, corner_id] = grads[1]
                    strain[3, 8 + corner_id] = grads[0]
                    strain[4, 8 + corner_id] = grads[2]
                    strain[4, 16 + corner_id] = grads[1]
                    strain[5, corner_id] = grads[2]
                    strain[5, 16 + corner_id] = grads[0]
                matrix = matrix + 0.125 * (strain.T @ elastic @ strain)
    return matrix.astype(np.float32)

def element_moduli(moduli_pad, extent_x, extent_y, depth):
    moduli_ext = jnp.concatenate([moduli_pad, jnp.zeros(moduli_pad.shape[:2] + (1,), moduli_pad.dtype)], axis=2)
    total = jnp.zeros((extent_x + 1, extent_y + 1, depth), moduli_pad.dtype)
    for shift_x, shift_y, shift_z in CORNER_LIST:
        total = total + moduli_ext[shift_x:shift_x + extent_x + 1, shift_y:shift_y + extent_y + 1, shift_z:shift_z + depth]
    return 0.125 * total

def assemble(forces, extent_x, extent_y):
    depth = forces.shape[4]
    result = jnp.zeros((3, extent_x, extent_y, depth), forces.dtype)
    for corner_id in range(8):
        shift_x, shift_y, shift_z = CORNER_LIST[corner_id]
        piece = forces[:, corner_id, 1 - shift_x:1 - shift_x + extent_x, 1 - shift_y:1 - shift_y + extent_y, :]
        if shift_z:
            piece = jnp.concatenate([jnp.zeros_like(piece[..., :1]), piece[..., :-1]], axis=3)
        result = result + piece
    return result

def slab_forces(padded, moduli_pad, stiffness):
    extent_x = padded.shape[1] - 2
    extent_y = padded.shape[2] - 2
    depth = padded.shape[3]
    field = jnp.concatenate([padded, jnp.zeros(padded.shape[:3] + (1,), padded.dtype)], axis=3)
    pieces = []
    for shift_x, shift_y, shift_z in CORNER_LIST:
        pieces.append(field[:, shift_x:shift_x + extent_x + 1, shift_y:shift_y + extent_y + 1, shift_z:shift_z + depth])
    stacked = jnp.stack(pieces, axis=1).reshape((24, extent_x + 1, extent_y + 1, depth))
    modulus = element_moduli(moduli_pad, extent_x, extent_y, depth)
    forces = jnp.einsum('ij,jabc->iabc', stiffness, stacked, precision=lax.Precision.HIGHEST) * modulus
    return assemble(forces.reshape((3, 8, extent_x + 1, extent_y + 1, depth)), extent_x, extent_y)

def slab_diagonal(moduli_pad, entries):
    extent_x = moduli_pad.shape[0] - 2
    extent_y = moduli_pad.shape[1] - 2
    depth = moduli_pad.shape[2]
    modulus = element_moduli(moduli_pad, extent_x, extent_y, depth)
    forces = entries[:, None, None, None] * modulus
    return assemble(forces.reshape((3, 8, extent_x + 1, extent_y + 1, depth)), extent_x, extent_y)

def stiffness_apply(padded, moduli_pad, stiffness, slab):
    extent_x = padded.shape[1] - 2
    count = extent_x // slab

    def one_slab(block):
        start = block * slab
        part_field = lax.dynamic_slice_in_dim(padded, start, slab + 2, 1)
        part_moduli = lax.dynamic_slice_in_dim(moduli_pad, start, slab + 2, 0)
        return slab_forces(part_field, part_moduli, stiffness)
    blocks = lax.map(one_slab, jnp.arange(count, dtype=jnp.int32))
    return jnp.moveaxis(blocks, 0, 1).reshape((3, extent_x) + blocks.shape[3:])

def stiffness_diagonal(moduli_pad, entries, slab):
    extent_x = moduli_pad.shape[0] - 2
    count = extent_x // slab

    def one_slab(block):
        start = block * slab
        part_moduli = lax.dynamic_slice_in_dim(moduli_pad, start, slab + 2, 0)
        return slab_diagonal(part_moduli, entries)
    blocks = lax.map(one_slab, jnp.arange(count, dtype=jnp.int32))
    return jnp.moveaxis(blocks, 0, 1).reshape((3, extent_x) + blocks.shape[3:])

def reference(rhs_force, moduli, fixed_nodes, contact_nodes):
    stiffness = jnp.asarray(element_matrix(), dtype=jnp.float32)
    entries = jnp.diagonal(stiffness)
    fixed = fixed_nodes.astype(jnp.float32)
    free = 1.0 - fixed
    contact = contact_nodes.astype(jnp.float32) * PENALTY
    moduli_pad = jnp.pad(moduli, ((1, 1), (1, 1), (0, 0)))
    slab = math.gcd(NX, 32)
    diag = free * (stiffness_diagonal(moduli_pad, entries, slab) + contact) + fixed

    def operate(field):
        padded = jnp.pad(field, ((0, 0), (1, 1), (1, 1), (0, 0)))
        return free * (stiffness_apply(padded, moduli_pad, stiffness, slab) + contact * field) + fixed * field
    solution = jnp.zeros_like(rhs_force)
    residual = free * rhs_force
    precond = residual / diag
    direction = precond
    norm_now = jnp.sum(residual * precond)
    for step in range(ITERS):
        image = operate(direction)
        alpha = norm_now / jnp.sum(direction * image)
        solution = solution + alpha * direction
        residual = residual - alpha * image
        if step + 1 < ITERS:
            precond = residual / diag
            norm_next = jnp.sum(residual * precond)
            direction = precond + norm_next / norm_now * direction
            norm_now = norm_next
    return (solution, residual)
```

```python
import math

import jax
import jax.numpy as jnp
import numpy as np
from jax import lax
from jax.sharding import PartitionSpec as P

ITERS = 3
DIG = ("x", "z", "core")
DIG_SIZES = (4, 12, 2)


POISSON = 0.3
PENALTY = 6.0
CORNER_LIST = (
    (0, 0, 0),
    (0, 0, 1),
    (0, 1, 0),
    (0, 1, 1),
    (1, 0, 0),
    (1, 0, 1),
    (1, 1, 0),
    (1, 1, 1),
)


def neighbours(axis, low_part, high_part):
    count = math.prod(lax.axis_size(name) for name in axis)
    forward = [(i, i + 1) for i in range(count - 1)]
    backward = [(target, source) for source, target in forward]
    return lax.ppermute(high_part, axis, forward), lax.ppermute(low_part, axis, backward)


def element_matrix():
    lame_first = POISSON / ((1.0 + POISSON) * (1.0 - 2.0 * POISSON))
    shear = 0.5 / (1.0 + POISSON)
    elastic = np.zeros((6, 6))
    elastic[:3, :3] = lame_first
    for dim_one in range(3):
        elastic[dim_one, dim_one] += 2.0 * shear
        elastic[dim_one + 3, dim_one + 3] = shear
    points = (0.5 - 0.5 / math.sqrt(3.0), 0.5 + 0.5 / math.sqrt(3.0))
    matrix = np.zeros((24, 24))
    for point_x in points:
        for point_y in points:
            for point_z in points:
                coords = (point_x, point_y, point_z)
                strain = np.zeros((6, 24))
                for corner_id in range(8):
                    corner = CORNER_LIST[corner_id]
                    grads = []
                    for dim_one in range(3):
                        product = 1.0
                        for dim_two in range(3):
                            if dim_two == dim_one:
                                factor = 1.0 if corner[dim_two] else -1.0
                            else:
                                factor = (
                                    coords[dim_two] if corner[dim_two] else 1.0 - coords[dim_two]
                                )
                            product = product * factor
                        grads.append(product)
                    for dim_one in range(3):
                        strain[dim_one, dim_one * 8 + corner_id] = grads[dim_one]
                    strain[3, corner_id] = grads[1]
                    strain[3, 8 + corner_id] = grads[0]
                    strain[4, 8 + corner_id] = grads[2]
                    strain[4, 16 + corner_id] = grads[1]
                    strain[5, corner_id] = grads[2]
                    strain[5, 16 + corner_id] = grads[0]
                matrix = matrix + 0.125 * (strain.T @ elastic @ strain)
    return matrix.astype(np.float32)


def element_moduli(moduli_pad, extent_x, extent_y, depth):
    moduli_ext = jnp.concatenate(
        [moduli_pad, jnp.zeros(moduli_pad.shape[:2] + (1,), moduli_pad.dtype)], axis=2
    )
    total = jnp.zeros((extent_x + 1, extent_y + 1, depth), moduli_pad.dtype)
    for shift_x, shift_y, shift_z in CORNER_LIST:
        total = (
            total
            + moduli_ext[
                shift_x : shift_x + extent_x + 1,
                shift_y : shift_y + extent_y + 1,
                shift_z : shift_z + depth,
            ]
        )
    return 0.125 * total


def assemble(forces, extent_x, extent_y):
    depth = forces.shape[4]
    result = jnp.zeros((3, extent_x, extent_y, depth), forces.dtype)
    for corner_id in range(8):
        shift_x, shift_y, shift_z = CORNER_LIST[corner_id]
        piece = forces[
            :,
            corner_id,
            1 - shift_x : 1 - shift_x + extent_x,
            1 - shift_y : 1 - shift_y + extent_y,
            :,
        ]
        if shift_z:
            piece = jnp.concatenate([jnp.zeros_like(piece[..., :1]), piece[..., :-1]], axis=3)
        result = result + piece
    return result


def slab_forces(padded, moduli_pad, stiffness):
    extent_x = padded.shape[1] - 2
    extent_y = padded.shape[2] - 2
    depth = padded.shape[3]
    field = jnp.concatenate([padded, jnp.zeros(padded.shape[:3] + (1,), padded.dtype)], axis=3)
    pieces = []
    for shift_x, shift_y, shift_z in CORNER_LIST:
        pieces.append(
            field[
                :,
                shift_x : shift_x + extent_x + 1,
                shift_y : shift_y + extent_y + 1,
                shift_z : shift_z + depth,
            ]
        )
    stacked = jnp.stack(pieces, axis=1).reshape((24, extent_x + 1, extent_y + 1, depth))
    modulus = element_moduli(moduli_pad, extent_x, extent_y, depth)
    forces = (
        jnp.einsum("ij,jabc->iabc", stiffness, stacked, precision=lax.Precision.HIGHEST) * modulus
    )
    return assemble(forces.reshape((3, 8, extent_x + 1, extent_y + 1, depth)), extent_x, extent_y)


def slab_diagonal(moduli_pad, entries):
    extent_x = moduli_pad.shape[0] - 2
    extent_y = moduli_pad.shape[1] - 2
    depth = moduli_pad.shape[2]
    modulus = element_moduli(moduli_pad, extent_x, extent_y, depth)
    forces = entries[:, None, None, None] * modulus
    return assemble(forces.reshape((3, 8, extent_x + 1, extent_y + 1, depth)), extent_x, extent_y)


def deep_halo(field, moduli):
    planes = field.shape[1]
    count = field.shape[0] * planes
    both = jnp.concatenate([field.reshape((count,) + field.shape[2:]), moduli], axis=0)
    low, high = neighbours(("cross",), both[:, :4], both[:, -4:])
    both = jnp.concatenate([low, both, high], axis=1)
    field = both[:count].reshape((field.shape[0], planes) + both.shape[1:])
    moduli = both[count:]

    def packed(part):
        return jnp.concatenate([part.reshape((-1,) + part.shape[2:]), moduli], axis=0)

    def parted(block):
        return block[:-planes].reshape((field.shape[0], -1) + block.shape[1:]), block[-planes:]

    low, high = neighbours(DIG, packed(field[:, :3]), packed(field[:, -3:]))
    low_field, low_moduli = parted(low)
    high_field, high_moduli = parted(high)
    field = jnp.concatenate([low_field, field, high_field], axis=1)
    return field, jnp.concatenate([low_moduli, moduli, high_moduli], axis=0)


def global_sum(value):
    for axis in ("core", "x", "cross", "z"):
        value = lax.psum(value, axis)
    return value


def dot_moments(moments, left, right, shift):
    total = 0.0
    for i, a in enumerate(left):
        for j, b in enumerate(right):
            total = total + a * b * moments[i + j + shift]
    return total


def coefficients(moments):
    zero = jnp.zeros_like(moments[0])
    solution = [zero] * ITERS
    residual = [zero + 1.0] + [zero] * ITERS
    direction = [zero + 1.0] + [zero] * (ITERS - 1)
    norm_now = moments[0]
    for step in range(ITERS):
        used = direction[: step + 1]
        image = dot_moments(moments, used, used, 0) + dot_moments(moments, used, used, 1)
        alpha = norm_now / image
        for k in range(step + 1):
            solution[k] = solution[k] + alpha * direction[k]
            residual[k] = residual[k] - alpha * direction[k]
        for k in range(step + 1):
            residual[k + 1] = residual[k + 1] - alpha * direction[k]
        if step + 1 < ITERS:
            used = residual[: step + 2]
            norm_next = dot_moments(moments, used, used, 0)
            beta = norm_next / norm_now
            for k in range(step + 2):
                direction[k] = residual[k] + beta * direction[k]
            norm_now = norm_next
    return solution, residual


def local(rhs_force, moduli, fixed_nodes, contact_nodes):
    stiffness = jnp.asarray(element_matrix(), dtype=jnp.float32)
    entries = jnp.diagonal(stiffness)
    free = 1.0 - fixed_nodes.astype(jnp.float32)
    contact = contact_nodes.astype(jnp.float32) * PENALTY
    field = jnp.concatenate([free * rhs_force, free[None], contact[None]], axis=0)
    field, moduli_pad = deep_halo(field, moduli)
    field = field[:, :, 1:-1]
    residual, free, contact = field[:3], field[3], field[4]
    keep = free * contact + (1.0 - free)
    diag = free * slab_diagonal(moduli_pad, entries) + keep
    bases = [residual / diag]
    images = [residual]
    for step in range(ITERS):
        moduli_pad = moduli_pad[1:-1, 1:-1]
        free, keep = free[1:-1, 1:-1], keep[1:-1, 1:-1]
        vector = bases[-1]
        image = free * slab_forces(vector, moduli_pad, stiffness) + keep * vector[:, 1:-1, 1:-1]
        images.append(image - images[-1][:, 1:-1, 1:-1])
        if step + 1 < ITERS:
            diag = diag[:, 1:-1, 1:-1]
            bases.append(images[-1] / diag)

    def own(value):
        edge_x = (value.shape[1] - rhs_force.shape[1]) // 2
        edge_y = (value.shape[2] - rhs_force.shape[2]) // 2
        return value[:, edge_x : value.shape[1] - edge_x, edge_y : value.shape[2] - edge_y]

    bases = [own(value) for value in bases]
    images = [own(value) for value in images]
    sums = [jnp.sum(bases[k // 2] * images[(k + 1) // 2]) for k in range(2 * ITERS)]
    moments = global_sum(jnp.stack(sums))
    moments = [moments[k] for k in range(2 * ITERS)]
    along, left = coefficients(moments)
    solution = sum(factor * value for factor, value in zip(along, bases))
    residual = sum(factor * value for factor, value in zip(left, images))
    return (solution, residual)


def solution(mesh):
    parts = DIG_SIZES + (mesh.shape["cross"],)
    split = jax.sharding.Mesh(mesh.devices.reshape(parts), DIG + ("cross",))
    return jax.shard_map(
        local,
        mesh=split,
        in_specs=(
            P(None, DIG, "cross", None),
            P(DIG, "cross", None),
            P(DIG, "cross", None),
            P(DIG, "cross", None),
        ),
        out_specs=(P(None, DIG, "cross", None), P(None, DIG, "cross", None)),
        check_vma=False,
    )
```

```python
import math

import jax
import jax.numpy as jnp
from jax import lax
from jax.experimental import pallas as pl
from jax.experimental.pallas import tpu as pltpu
from jax.sharding import PartitionSpec as P

ITERS = 3
POISSON = 0.3
PENALTY = 6.0
LAME_FIRST = POISSON / ((1.0 + POISSON) * (1.0 - 2.0 * POISSON))
SHEAR = 0.5 / (1.0 + POISSON)
ENTRY = (LAME_FIRST + 4.0 * SHEAR) / 9.0
RATIO = 2.0 * POISSON / (1.0 - 2.0 * POISSON)
DIG = ("x", "z", "core")
DIG_SIZES = (4, 12, 2)
PLANES = 4
ROWS = 8
EDGE = 4
DEEP = 3
FIELDS = 5
TALL = ROWS + 2 * EDGE


def up_z(value):
    depth = value.shape[1]
    lane = lax.broadcasted_iota(jnp.int32, value.shape, 1)
    return jnp.where(lane == depth - 1, 0.0, pltpu.roll(value, depth - 1, 1))


def down_z(value):
    lane = lax.broadcasted_iota(jnp.int32, value.shape, 1)
    return jnp.where(lane == 0, 0.0, pltpu.roll(value, 1, 1))


def up_y(value):
    return pltpu.roll(value, value.shape[0] - 1, 0)


def down_y(value):
    return pltpu.roll(value, 1, 0)


def node_modes(value):
    beyond = up_z(value)
    plus, minus = value + beyond, beyond - value
    plus_up, minus_up = up_y(plus), up_y(minus)
    return {
        "ss": plus + plus_up,
        "ds": plus_up - plus,
        "sd": minus + minus_up,
        "dd": minus_up - minus,
    }


def element_stress(low, high, weights):
    strain = []
    for component in range(3):
        modes = {}
        for name in ("ss", "ds", "sd", "dd"):
            modes["d" + name] = high[component][name] - low[component][name]
            if name != "ss":
                modes["s" + name] = high[component][name] + low[component][name]
        strain.append(modes)
    u, v, w = strain
    whole, third, ninth = weights
    trace = RATIO * (u["dss"] + v["sds"] + w["ssd"])
    xy = whole * (u["sds"] + v["dss"])
    xz = whole * (u["ssd"] + w["dss"])
    yz = whole * (v["ssd"] + w["sds"])

    def normal(value):
        return whole * (value + value + trace)

    def pair(one, other):
        half = 0.5 * (one + other)
        return whole * (one + half), whole * (other + half)

    u_dsd, v_sdd = pair(u["dsd"], v["sdd"])
    u_dds, w_sdd = pair(u["dds"], w["sdd"])
    v_dds, w_dsd = pair(v["dds"], w["dsd"])
    twist = u["sdd"] + v["dsd"] + w["dds"]
    return (
        {
            "dss": normal(u["dss"]),
            "sds": xy,
            "ssd": xz,
            "dsd": u_dsd,
            "dds": u_dds,
            "sdd": third * (twist + u["sdd"]),
            "ddd": ninth * u["ddd"],
        },
        {
            "sds": normal(v["sds"]),
            "dss": xy,
            "ssd": yz,
            "sdd": v_sdd,
            "dds": v_dds,
            "dsd": third * (twist + v["dsd"]),
            "ddd": ninth * v["ddd"],
        },
        {
            "ssd": normal(w["ssd"]),
            "dss": xz,
            "sds": yz,
            "sdd": w_sdd,
            "dsd": w_dsd,
            "dds": third * (twist + w["dds"]),
            "ddd": ninth * w["ddd"],
        },
    )


def node_force(low, high):
    total = {"ss": low["dss"] - high["dss"]}
    for name in ("ds", "sd", "dd"):
        total[name] = (low["s" + name] + low["d" + name]) + (high["s" + name] - high["d" + name])
    plus = (total["ss"] - total["ds"]) + down_y(total["ss"] + total["ds"])
    minus = (total["sd"] - total["dd"]) + down_y(total["sd"] + total["dd"])
    return (plus - minus) + down_z(plus + minus)


def rows_kernel(force_ref, moduli_ref, fixed_ref, contact_ref, both_ref, low_ref, high_ref):
    for plane in range(PLANES):
        free = 1.0 - fixed_ref[plane].astype(jnp.float32)
        contact = PENALTY * contact_ref[plane].astype(jnp.float32)
        packed = [free * force_ref[component, plane] for component in range(3)]
        packed += [free, contact, moduli_ref[plane]]
        for field, value in enumerate(packed):
            spot = field * PLANES + plane
            both_ref[spot] = value
            low_ref[spot] = value[:EDGE]
            high_ref[spot] = value[ROWS - EDGE :]


def planes_kernel(both_ref, below_ref, above_ref, tall_ref, low_ref, high_ref):
    for field in range(FIELDS + 1):
        for plane in range(PLANES):
            spot = field * PLANES + plane
            value = jnp.concatenate([below_ref[spot], both_ref[spot], above_ref[spot]], axis=0)
            tall_ref[spot] = value
            if field == FIELDS:
                low_ref[FIELDS * DEEP + plane] = value
                high_ref[FIELDS * DEEP + plane] = value
            else:
                if plane < DEEP:
                    low_ref[field * DEEP + plane] = value
                if plane >= PLANES - DEEP:
                    high_ref[field * DEEP + plane - PLANES + DEEP] = value


def krylov_kernel(tall_ref, below_ref, above_ref, image_ref, inverse_ref, moment_ref):
    def plane_of(field, plane):
        deep = PLANES if field == FIELDS else DEEP
        if plane < 0:
            return below_ref[field * DEEP + plane + deep]
        if plane >= PLANES:
            return above_ref[field * DEEP + plane - PLANES]
        return tall_ref[field * PLANES + plane]

    def own(value):
        return value[EDGE : EDGE + ROWS]

    columns = {}
    for plane in range(-PLANES, 2 * PLANES):
        value = plane_of(FIELDS, plane)
        value = value + up_z(value)
        columns[plane] = value + up_y(value)
    whole = {
        plane: (0.125 * SHEAR / 16.0) * (columns[plane] + columns[plane + 1])
        for plane in range(-PLANES, 2 * PLANES - 1)
    }
    free, keep, inverse = {}, {}, {}
    image = {}
    for plane in range(-DEEP, PLANES + DEEP):
        free[plane] = plane_of(3, plane)
        keep[plane] = free[plane] * plane_of(4, plane) + (1.0 - free[plane])
        value = whole[plane - 1] + whole[plane]
        value = value + down_y(value)
        value = (ENTRY * 16.0 / SHEAR) * (value + down_z(value))
        inverse[plane] = 1.0 / (free[plane] * value + keep[plane])
        for component in range(3):
            image[component, plane] = plane_of(component, plane)
    row = lax.broadcasted_iota(jnp.int32, image[0, 0].shape, 0)
    mine = (row >= EDGE) & (row < EDGE + ROWS)
    moments = []

    def moment(left, right):
        total = 0.0
        for component in range(3):
            for plane in range(PLANES):
                total = total + left[component, plane] * right[component, plane]
        total = jnp.where(mine, total, 0.0)
        moments.append(jnp.sum(total, axis=0, keepdims=True))

    for plane in range(PLANES):
        inverse_ref[plane] = own(inverse[plane])
    for step in range(ITERS + 1):
        for component in range(3):
            for plane in range(PLANES):
                image_ref[step, component * PLANES + plane] = own(image[component, plane])
        if step:
            moment(vector, image)
        if step == ITERS:
            break
        reach = DEEP - step
        vector = {
            (component, plane): image[component, plane] * inverse[plane]
            for component in range(3)
            for plane in range(-reach, PLANES + reach)
        }
        moment(vector, image)
        following = {}
        for plane in range(-reach, PLANES + reach):
            modes = [node_modes(vector[component, plane]) for component in range(3)]
            if plane > -reach:
                scale = whole[plane - 1]
                stress = element_stress(
                    before, modes, (scale, scale * (1.0 / 3.0), scale * (5.5 / 9.0))
                )
                if plane > 1 - reach:
                    node = plane - 1
                    for component in range(3):
                        force = node_force(earlier[component], stress[component])
                        here = vector[component, node]
                        following[component, node] = (
                            free[node] * force + keep[node] * here
                        ) - image[component, node]
                earlier = stress
            before = modes
        image = following
    stacked = jnp.concatenate(moments + [jnp.zeros_like(moments[0])] * (8 - len(moments)), axis=0)
    total = jnp.sum(stacked, axis=1, keepdims=True)
    moment_ref[...] = jnp.broadcast_to(total, moment_ref.shape)


def dot_moments(moments, left, right, shift):
    total = 0.0
    for i, a in enumerate(left):
        for j, b in enumerate(right):
            total = total + a * b * moments[i + j + shift]
    return total


def coefficients(moments):
    zero = jnp.zeros_like(moments[0])
    solution = [zero] * ITERS
    residual = [zero + 1.0] + [zero] * ITERS
    direction = [zero + 1.0] + [zero] * (ITERS - 1)
    norm_now = moments[0]
    for step in range(ITERS):
        used = direction[: step + 1]
        image = dot_moments(moments, used, used, 0) + dot_moments(moments, used, used, 1)
        alpha = norm_now / image
        for k in range(step + 1):
            solution[k] = solution[k] + alpha * direction[k]
            residual[k] = residual[k] - alpha * direction[k]
        for k in range(step + 1):
            residual[k + 1] = residual[k + 1] - alpha * direction[k]
        if step + 1 < ITERS:
            used = residual[: step + 2]
            norm_next = dot_moments(moments, used, used, 0)
            beta = norm_next / norm_now
            for k in range(step + 2):
                direction[k] = residual[k] + beta * direction[k]
            norm_now = norm_next
    return solution, residual


def finish_kernel(image_ref, inverse_ref, moment_ref, solution_ref, residual_ref):
    moments = [moment_ref[k : k + 1] for k in range(2 * ITERS)]
    along, left = coefficients(moments)
    depth = image_ref.shape[-1]
    reps = depth // moment_ref.shape[-1]

    def spread(value):
        value = jnp.broadcast_to(value, (ROWS, value.shape[1]))
        return jnp.concatenate([value] * reps, axis=1)

    along = [spread(value) for value in along]
    left = [spread(value) for value in left]
    for component in range(3):
        for plane in range(PLANES):
            spot = component * PLANES + plane
            images = [image_ref[k, spot] for k in range(ITERS + 1)]
            value = sum(a * b for a, b in zip(along, images[:ITERS]))
            solution_ref[component, plane] = value * inverse_ref[plane]
            residual_ref[component, plane] = sum(a * b for a, b in zip(left, images))


def shaped(*shape):
    return jax.ShapeDtypeStruct(shape, jnp.float32)


def neighbours(axis, low_part, high_part):
    count = math.prod(lax.axis_size(name) for name in axis)
    forward = [(i, i + 1) for i in range(count - 1)]
    backward = [(target, source) for source, target in forward]
    return lax.ppermute(high_part, axis, forward), lax.ppermute(low_part, axis, backward)


def global_sum(value):
    for axis in ("core", "x", "cross", "z"):
        value = lax.psum(value, axis)
    return value


def call(kernel, outs, *args):
    return pl.pallas_call(
        kernel,
        out_shape=outs,
        compiler_params=pltpu.CompilerParams(vmem_limit_bytes=32 << 20),
    )(*args)


def local(rhs_force, moduli, fixed_nodes, contact_nodes):
    depth = rhs_force.shape[3]
    count = (FIELDS + 1) * PLANES
    edge = shaped(count, EDGE, depth)
    both, low, high = call(
        rows_kernel,
        (shaped(count, ROWS, depth), edge, edge),
        rhs_force,
        moduli,
        fixed_nodes,
        contact_nodes,
    )
    below, above = neighbours(("cross",), low, high)
    edge = shaped(FIELDS * DEEP + PLANES, TALL, depth)
    tall, low, high = call(
        planes_kernel, (shaped(count, TALL, depth), edge, edge), both, below, above
    )
    below, above = neighbours(DIG, low, high)
    image, inverse, moments = call(
        krylov_kernel,
        (
            shaped(ITERS + 1, 3 * PLANES, ROWS, depth),
            shaped(PLANES, ROWS, depth),
            shaped(8, 128),
        ),
        tall,
        below,
        above,
    )
    moments = global_sum(moments)
    out = shaped(3, PLANES, ROWS, depth)
    return tuple(call(finish_kernel, (out, out), image, inverse, moments))


def solution(mesh):
    parts = DIG_SIZES + (mesh.shape["cross"],)
    split = jax.sharding.Mesh(mesh.devices.reshape(parts), DIG + ("cross",))
    return jax.shard_map(
        local,
        mesh=split,
        in_specs=(
            P(None, DIG, "cross", None),
            P(DIG, "cross", None),
            P(DIG, "cross", None),
            P(DIG, "cross", None),
        ),
        out_specs=(P(None, DIG, "cross", None), P(None, DIG, "cross", None)),
        check_vma=False,
    )
```

```python
import math

import jax
import jax.numpy as jnp
from jax import lax
from jax.experimental import pallas as pl
from jax.experimental.pallas import tpu as pltpu
from jax.sharding import PartitionSpec as P

ITERS = 3
POISSON = 0.3
PENALTY = 6.0
LAME_FIRST = POISSON / ((1.0 + POISSON) * (1.0 - 2.0 * POISSON))
SHEAR = 0.5 / (1.0 + POISSON)
ENTRY = (LAME_FIRST + 4.0 * SHEAR) / 9.0
RATIO = 2.0 * POISSON / (1.0 - 2.0 * POISSON)
DIG = ("x", "z", "core")
DIG_SIZES = (4, 12, 2)
SUM_FIRST = ("x", "core", "cross")
SUM_LAST = ("z",)
PLANES = 4
ROWS = 8
EDGE = 4
DEEP = 3
FIELDS = 5
TALL = ROWS + 2 * EDGE


def up_z(value):
    depth = value.shape[1]
    lane = lax.broadcasted_iota(jnp.int32, value.shape, 1)
    return jnp.where(lane == depth - 1, 0.0, pltpu.roll(value, depth - 1, 1))


def down_z(value):
    lane = lax.broadcasted_iota(jnp.int32, value.shape, 1)
    return jnp.where(lane == 0, 0.0, pltpu.roll(value, 1, 1))


def up_y(value):
    return pltpu.roll(value, value.shape[0] - 1, 0)


def down_y(value):
    return pltpu.roll(value, 1, 0)


def node_modes(value):
    beyond = up_z(value)
    plus, minus = value + beyond, beyond - value
    plus_up, minus_up = up_y(plus), up_y(minus)
    return {
        "ss": plus + plus_up,
        "ds": plus_up - plus,
        "sd": minus + minus_up,
        "dd": minus_up - minus,
    }


def element_stress(low, high, weights):
    strain = []
    for component in range(3):
        modes = {}
        for name in ("ss", "ds", "sd", "dd"):
            modes["d" + name] = high[component][name] - low[component][name]
            if name != "ss":
                modes["s" + name] = high[component][name] + low[component][name]
        strain.append(modes)
    u, v, w = strain
    whole, third, ninth = weights
    trace = RATIO * (u["dss"] + v["sds"] + w["ssd"])
    xy = whole * (u["sds"] + v["dss"])
    xz = whole * (u["ssd"] + w["dss"])
    yz = whole * (v["ssd"] + w["sds"])

    def normal(value):
        return whole * (value + value + trace)

    def pair(one, other):
        half = 0.5 * (one + other)
        return whole * (one + half), whole * (other + half)

    u_dsd, v_sdd = pair(u["dsd"], v["sdd"])
    u_dds, w_sdd = pair(u["dds"], w["sdd"])
    v_dds, w_dsd = pair(v["dds"], w["dsd"])
    twist = u["sdd"] + v["dsd"] + w["dds"]
    return (
        {
            "dss": normal(u["dss"]),
            "sds": xy,
            "ssd": xz,
            "dsd": u_dsd,
            "dds": u_dds,
            "sdd": third * (twist + u["sdd"]),
            "ddd": ninth * u["ddd"],
        },
        {
            "sds": normal(v["sds"]),
            "dss": xy,
            "ssd": yz,
            "sdd": v_sdd,
            "dds": v_dds,
            "dsd": third * (twist + v["dsd"]),
            "ddd": ninth * v["ddd"],
        },
        {
            "ssd": normal(w["ssd"]),
            "dss": xz,
            "sds": yz,
            "sdd": w_sdd,
            "dsd": w_dsd,
            "dds": third * (twist + w["dds"]),
            "ddd": ninth * w["ddd"],
        },
    )


def node_force(low, high):
    total = {"ss": low["dss"] - high["dss"]}
    for name in ("ds", "sd", "dd"):
        total[name] = (low["s" + name] + low["d" + name]) + (high["s" + name] - high["d" + name])
    plus = (total["ss"] - total["ds"]) + down_y(total["ss"] + total["ds"])
    minus = (total["sd"] - total["dd"]) + down_y(total["sd"] + total["dd"])
    return (plus - minus) + down_z(plus + minus)


def rows_kernel(*refs):
    arguments, (both_ref, low_ref, high_ref) = refs[:4], refs[4:7]
    buffers, arrived = refs[7:11], refs[11]
    copies = [
        pltpu.make_async_copy(source, target, arrived.at[k])
        for k, (source, target) in enumerate(zip(arguments, buffers))
    ]
    for copy in copies:
        copy.start()
    for copy in copies:
        copy.wait()
    force_ref, moduli_ref, fixed_ref, contact_ref = buffers
    for plane in range(PLANES):
        free = 1.0 - fixed_ref[plane].astype(jnp.float32)
        contact = PENALTY * contact_ref[plane].astype(jnp.float32)
        packed = [free * force_ref[component, plane] for component in range(3)]
        packed += [free, contact, moduli_ref[plane]]
        for field, value in enumerate(packed):
            spot = field * PLANES + plane
            both_ref[spot] = value
            low_ref[spot] = value[:EDGE]
            high_ref[spot] = value[ROWS - EDGE :]


def planes_kernel(both_ref, below_ref, above_ref, tall_ref, low_ref, high_ref):
    for field in range(FIELDS + 1):
        for plane in range(PLANES):
            spot = field * PLANES + plane
            value = jnp.concatenate([below_ref[spot], both_ref[spot], above_ref[spot]], axis=0)
            tall_ref[spot] = value
            if field == FIELDS:
                low_ref[FIELDS * DEEP + plane] = value
                high_ref[FIELDS * DEEP + plane] = value
            else:
                if plane < DEEP:
                    low_ref[field * DEEP + plane] = value
                if plane >= PLANES - DEEP:
                    high_ref[field * DEEP + plane - PLANES + DEEP] = value


def krylov_kernel(tall_ref, below_ref, above_ref, image_ref, inverse_ref, moment_ref):
    def plane_of(field, plane):
        deep = PLANES if field == FIELDS else DEEP
        if plane < 0:
            return below_ref[field * DEEP + plane + deep]
        if plane >= PLANES:
            return above_ref[field * DEEP + plane - PLANES]
        return tall_ref[field * PLANES + plane]

    def own(value):
        return value[EDGE : EDGE + ROWS]

    columns = {}
    for plane in range(-PLANES, 2 * PLANES):
        value = plane_of(FIELDS, plane)
        value = value + up_z(value)
        columns[plane] = value + up_y(value)
    whole = {
        plane: (0.125 * SHEAR / 16.0) * (columns[plane] + columns[plane + 1])
        for plane in range(-PLANES, 2 * PLANES - 1)
    }
    free, keep, inverse = {}, {}, {}
    image = {}
    for plane in range(-DEEP, PLANES + DEEP):
        free[plane] = plane_of(3, plane)
        keep[plane] = free[plane] * plane_of(4, plane) + (1.0 - free[plane])
        value = whole[plane - 1] + whole[plane]
        value = value + down_y(value)
        value = (ENTRY * 16.0 / SHEAR) * (value + down_z(value))
        inverse[plane] = 1.0 / (free[plane] * value + keep[plane])
        for component in range(3):
            image[component, plane] = plane_of(component, plane)
    row = lax.broadcasted_iota(jnp.int32, image[0, 0].shape, 0)
    mine = (row >= EDGE) & (row < EDGE + ROWS)
    moments = []

    def moment(left, right):
        total = 0.0
        for component in range(3):
            for plane in range(PLANES):
                total = total + left[component, plane] * right[component, plane]
        total = jnp.where(mine, total, 0.0)
        moments.append(jnp.sum(total, axis=0, keepdims=True))

    for plane in range(PLANES):
        inverse_ref[plane] = own(inverse[plane])
    for step in range(ITERS + 1):
        for component in range(3):
            for plane in range(PLANES):
                image_ref[step, component * PLANES + plane] = own(image[component, plane])
        if step:
            moment(vector, image)
        if step == ITERS:
            break
        reach = DEEP - step
        vector = {
            (component, plane): image[component, plane] * inverse[plane]
            for component in range(3)
            for plane in range(-reach, PLANES + reach)
        }
        moment(vector, image)
        following = {}
        for plane in range(-reach, PLANES + reach):
            modes = [node_modes(vector[component, plane]) for component in range(3)]
            if plane > -reach:
                scale = whole[plane - 1]
                stress = element_stress(
                    before, modes, (scale, scale * (1.0 / 3.0), scale * (5.5 / 9.0))
                )
                if plane > 1 - reach:
                    node = plane - 1
                    for component in range(3):
                        force = node_force(earlier[component], stress[component])
                        here = vector[component, node]
                        following[component, node] = (
                            free[node] * force + keep[node] * here
                        ) - image[component, node]
                earlier = stress
            before = modes
        image = following
    stacked = jnp.concatenate(moments + [jnp.zeros_like(moments[0])] * (8 - len(moments)), axis=0)
    total = jnp.broadcast_to(jnp.sum(stacked, axis=1, keepdims=True), (8, 128))
    chosen = lax.broadcasted_iota(jnp.int32, (8, 128), 0) == lax.broadcasted_iota(
        jnp.int32, (8, 128), 1
    )
    total = jnp.sum(jnp.where(chosen, total, 0.0), axis=0, keepdims=True)
    moment_ref[...] = jnp.broadcast_to(total, moment_ref.shape)


def sum_kernel(part_ref, total_ref):
    total = jnp.sum(part_ref[...], axis=0, keepdims=True)
    total_ref[...] = jnp.broadcast_to(total, total_ref.shape)


def dot_moments(moments, left, right, shift):
    total = 0.0
    for i, a in enumerate(left):
        for j, b in enumerate(right):
            total = total + a * b * moments[i + j + shift]
    return total


def coefficients(moments):
    zero = jnp.zeros_like(moments[0])
    solution = [zero] * ITERS
    residual = [zero + 1.0] + [zero] * ITERS
    direction = [zero + 1.0] + [zero] * (ITERS - 1)
    norm_now = moments[0]
    for step in range(ITERS):
        used = direction[: step + 1]
        image = dot_moments(moments, used, used, 0) + dot_moments(moments, used, used, 1)
        alpha = norm_now / image
        for k in range(step + 1):
            solution[k] = solution[k] + alpha * direction[k]
            residual[k] = residual[k] - alpha * direction[k]
        for k in range(step + 1):
            residual[k + 1] = residual[k + 1] - alpha * direction[k]
        if step + 1 < ITERS:
            used = residual[: step + 2]
            norm_next = dot_moments(moments, used, used, 0)
            beta = norm_next / norm_now
            for k in range(step + 2):
                direction[k] = residual[k] + beta * direction[k]
            norm_now = norm_next
    return solution, residual


def finish_kernel(image_ref, inverse_ref, part_ref, solution_ref, residual_ref):
    total = jnp.sum(part_ref[...], axis=0, keepdims=True)
    moments = [jnp.broadcast_to(total[:, k : k + 1], total.shape) for k in range(2 * ITERS)]
    along, left = coefficients(moments)
    depth = image_ref.shape[-1]
    reps = depth // total.shape[1]

    def spread(value):
        value = jnp.broadcast_to(value, (ROWS, value.shape[1]))
        return jnp.concatenate([value] * reps, axis=1)

    along = [spread(value) for value in along]
    left = [spread(value) for value in left]
    for component in range(3):
        for plane in range(PLANES):
            spot = component * PLANES + plane
            images = [image_ref[k, spot] for k in range(ITERS + 1)]
            value = sum(a * b for a, b in zip(along, images[:ITERS]))
            solution_ref[component, plane] = value * inverse_ref[plane]
            residual_ref[component, plane] = sum(a * b for a, b in zip(left, images))


def shaped(*shape):
    return jax.ShapeDtypeStruct(shape, jnp.float32)


def neighbours(axis, low_part, high_part):
    count = math.prod(lax.axis_size(name) for name in axis)
    forward = [(i, i + 1) for i in range(count - 1)]
    backward = [(target, source) for source, target in forward]
    return lax.ppermute(high_part, axis, forward), lax.ppermute(low_part, axis, backward)


def members(axes):
    return math.prod(lax.axis_size(name) for name in axes)


def exchanged(rows, axes):
    return lax.all_to_all(rows, axes, 0, 0, tiled=True)


def call(kernel, outs, *args, **options):
    return pl.pallas_call(
        kernel,
        out_shape=outs,
        compiler_params=pltpu.CompilerParams(vmem_limit_bytes=32 << 20),
        **options,
    )(*args)


def local(rhs_force, moduli, fixed_nodes, contact_nodes):
    depth = rhs_force.shape[3]
    count = (FIELDS + 1) * PLANES
    edge = shaped(count, EDGE, depth)
    arguments = (rhs_force, moduli, fixed_nodes, contact_nodes)
    both, low, high = call(
        rows_kernel,
        (shaped(count, ROWS, depth), edge, edge),
        *arguments,
        in_specs=[pl.BlockSpec(memory_space=pl.ANY)] * len(arguments),
        scratch_shapes=[pltpu.VMEM(value.shape, value.dtype) for value in arguments]
        + [pltpu.SemaphoreType.DMA((len(arguments),))],
    )
    below, above = neighbours(("cross",), low, high)
    edge = shaped(FIELDS * DEEP + PLANES, TALL, depth)
    tall, low, high = call(
        planes_kernel, (shaped(count, TALL, depth), edge, edge), both, below, above
    )
    below, above = neighbours(DIG, low, high)
    image, inverse, moments = call(
        krylov_kernel,
        (
            shaped(ITERS + 1, 3 * PLANES, ROWS, depth),
            shaped(PLANES, ROWS, depth),
            shaped(members(SUM_FIRST), 128),
        ),
        tall,
        below,
        above,
    )
    moments = exchanged(moments, SUM_FIRST)
    moments = call(sum_kernel, shaped(members(SUM_LAST), 128), moments)
    moments = exchanged(moments, SUM_LAST)
    out = shaped(3, PLANES, ROWS, depth)
    return tuple(call(finish_kernel, (out, out), image, inverse, moments))


def solution(mesh):
    parts = DIG_SIZES + (mesh.shape["cross"],)
    split = jax.sharding.Mesh(mesh.devices.reshape(parts), DIG + ("cross",))
    return jax.shard_map(
        local,
        mesh=split,
        in_specs=(
            P(None, DIG, "cross", None),
            P(DIG, "cross", None),
            P(DIG, "cross", None),
            P(DIG, "cross", None),
        ),
        out_specs=(P(None, DIG, "cross", None), P(None, DIG, "cross", None)),
        check_vma=False,
    )
```

```python
import math

import jax
import jax.numpy as jnp
from jax import lax
from jax.experimental import pallas as pl
from jax.experimental.pallas import tpu as pltpu
from jax.sharding import PartitionSpec as P

ITERS = 3
POISSON = 0.3
PENALTY = 6.0
LAME_FIRST = POISSON / ((1.0 + POISSON) * (1.0 - 2.0 * POISSON))
SHEAR = 0.5 / (1.0 + POISSON)
ENTRY = (LAME_FIRST + 4.0 * SHEAR) / 9.0
RATIO = 2.0 * POISSON / (1.0 - 2.0 * POISSON)
DIG = ("x", "z", "core")
DIG_SIZES = (4, 12, 2)
SUM_FIRST = ("x", "cross")
SUM_LAST = ("z", "core")
PLANES = 4
ROWS = 8
EDGE = 4
DEEP = 3
FIELDS = 5
TALL = ROWS + 2 * EDGE


def up_z(value):
    depth = value.shape[1]
    lane = lax.broadcasted_iota(jnp.int32, value.shape, 1)
    return jnp.where(lane == depth - 1, 0.0, pltpu.roll(value, depth - 1, 1))


def down_z(value):
    lane = lax.broadcasted_iota(jnp.int32, value.shape, 1)
    return jnp.where(lane == 0, 0.0, pltpu.roll(value, 1, 1))


def up_y(value):
    return pltpu.roll(value, value.shape[0] - 1, 0)


def down_y(value):
    return pltpu.roll(value, 1, 0)


def node_modes(value):
    beyond = up_z(value)
    plus, minus = value + beyond, beyond - value
    plus_up, minus_up = up_y(plus), up_y(minus)
    return {
        "ss": plus + plus_up,
        "ds": plus_up - plus,
        "sd": minus + minus_up,
        "dd": minus_up - minus,
    }


def element_stress(low, high, weights):
    strain = []
    for component in range(3):
        modes = {}
        for name in ("ss", "ds", "sd", "dd"):
            modes["d" + name] = high[component][name] - low[component][name]
            if name != "ss":
                modes["s" + name] = high[component][name] + low[component][name]
        strain.append(modes)
    u, v, w = strain
    whole, third, ninth = weights
    trace = RATIO * (u["dss"] + v["sds"] + w["ssd"])
    xy = whole * (u["sds"] + v["dss"])
    xz = whole * (u["ssd"] + w["dss"])
    yz = whole * (v["ssd"] + w["sds"])

    def normal(value):
        return whole * (value + value + trace)

    def pair(one, other):
        half = 0.5 * (one + other)
        return whole * (one + half), whole * (other + half)

    u_dsd, v_sdd = pair(u["dsd"], v["sdd"])
    u_dds, w_sdd = pair(u["dds"], w["sdd"])
    v_dds, w_dsd = pair(v["dds"], w["dsd"])
    twist = u["sdd"] + v["dsd"] + w["dds"]
    return (
        {
            "dss": normal(u["dss"]),
            "sds": xy,
            "ssd": xz,
            "dsd": u_dsd,
            "dds": u_dds,
            "sdd": third * (twist + u["sdd"]),
            "ddd": ninth * u["ddd"],
        },
        {
            "sds": normal(v["sds"]),
            "dss": xy,
            "ssd": yz,
            "sdd": v_sdd,
            "dds": v_dds,
            "dsd": third * (twist + v["dsd"]),
            "ddd": ninth * v["ddd"],
        },
        {
            "ssd": normal(w["ssd"]),
            "dss": xz,
            "sds": yz,
            "sdd": w_sdd,
            "dsd": w_dsd,
            "dds": third * (twist + w["dds"]),
            "ddd": ninth * w["ddd"],
        },
    )


def node_force(low, high):
    total = {"ss": low["dss"] - high["dss"]}
    for name in ("ds", "sd", "dd"):
        total[name] = (low["s" + name] + low["d" + name]) + (high["s" + name] - high["d" + name])
    plus = (total["ss"] - total["ds"]) + down_y(total["ss"] + total["ds"])
    minus = (total["sd"] - total["dd"]) + down_y(total["sd"] + total["dd"])
    return (plus - minus) + down_z(plus + minus)


def rows_kernel(*refs):
    arguments, (both_ref, low_ref, high_ref) = refs[:4], refs[4:7]
    buffers, arrived = refs[7:11], refs[11]
    copies = [
        pltpu.make_async_copy(source, target, arrived.at[k])
        for k, (source, target) in enumerate(zip(arguments, buffers))
    ]
    for copy in copies:
        copy.start()
    for copy in copies:
        copy.wait()
    force_ref, moduli_ref, fixed_ref, contact_ref = buffers
    for plane in range(PLANES):
        free = 1.0 - fixed_ref[plane].astype(jnp.float32)
        contact = PENALTY * contact_ref[plane].astype(jnp.float32)
        packed = [free * force_ref[component, plane] for component in range(3)]
        packed += [free, contact, moduli_ref[plane]]
        for field, value in enumerate(packed):
            spot = field * PLANES + plane
            both_ref[spot] = value
            low_ref[spot] = value[:EDGE]
            high_ref[spot] = value[ROWS - EDGE :]


def planes_kernel(both_ref, below_ref, above_ref, tall_ref, low_ref, high_ref):
    for field in range(FIELDS + 1):
        for plane in range(PLANES):
            spot = field * PLANES + plane
            value = jnp.concatenate([below_ref[spot], both_ref[spot], above_ref[spot]], axis=0)
            tall_ref[spot] = value
            if field == FIELDS:
                low_ref[FIELDS * DEEP + plane] = value
                high_ref[FIELDS * DEEP + plane] = value
            else:
                if plane < DEEP:
                    low_ref[field * DEEP + plane] = value
                if plane >= PLANES - DEEP:
                    high_ref[field * DEEP + plane - PLANES + DEEP] = value


def krylov_kernel(tall_ref, below_ref, above_ref, image_ref, inverse_ref, moment_ref):
    def plane_of(field, plane):
        deep = PLANES if field == FIELDS else DEEP
        if plane < 0:
            return below_ref[field * DEEP + plane + deep]
        if plane >= PLANES:
            return above_ref[field * DEEP + plane - PLANES]
        return tall_ref[field * PLANES + plane]

    def own(value):
        return value[EDGE : EDGE + ROWS]

    columns = {}
    for plane in range(-PLANES, 2 * PLANES):
        value = plane_of(FIELDS, plane)
        value = value + up_z(value)
        columns[plane] = value + up_y(value)
    whole = {
        plane: (0.125 * SHEAR / 16.0) * (columns[plane] + columns[plane + 1])
        for plane in range(-PLANES, 2 * PLANES - 1)
    }
    free, keep, inverse = {}, {}, {}
    image = {}
    for plane in range(-DEEP, PLANES + DEEP):
        free[plane] = plane_of(3, plane)
        keep[plane] = free[plane] * plane_of(4, plane) + (1.0 - free[plane])
        value = whole[plane - 1] + whole[plane]
        value = value + down_y(value)
        value = (ENTRY * 16.0 / SHEAR) * (value + down_z(value))
        inverse[plane] = 1.0 / (free[plane] * value + keep[plane])
        for component in range(3):
            image[component, plane] = plane_of(component, plane)
    row = lax.broadcasted_iota(jnp.int32, image[0, 0].shape, 0)
    mine = (row >= EDGE) & (row < EDGE + ROWS)
    moments = []

    def moment(left, right):
        total = 0.0
        for component in range(3):
            for plane in range(PLANES):
                total = total + left[component, plane] * right[component, plane]
        total = jnp.where(mine, total, 0.0)
        moments.append(jnp.sum(total, axis=0, keepdims=True))

    for plane in range(PLANES):
        inverse_ref[plane] = own(inverse[plane])
    for step in range(ITERS + 1):
        for component in range(3):
            for plane in range(PLANES):
                image_ref[step, component * PLANES + plane] = own(image[component, plane])
        if step:
            moment(vector, image)
        if step == ITERS:
            break
        reach = DEEP - step
        vector = {
            (component, plane): image[component, plane] * inverse[plane]
            for component in range(3)
            for plane in range(-reach, PLANES + reach)
        }
        moment(vector, image)
        following = {}
        for plane in range(-reach, PLANES + reach):
            modes = [node_modes(vector[component, plane]) for component in range(3)]
            if plane > -reach:
                scale = whole[plane - 1]
                stress = element_stress(
                    before, modes, (scale, scale * (1.0 / 3.0), scale * (5.5 / 9.0))
                )
                if plane > 1 - reach:
                    node = plane - 1
                    for component in range(3):
                        force = node_force(earlier[component], stress[component])
                        here = vector[component, node]
                        following[component, node] = (
                            free[node] * force + keep[node] * here
                        ) - image[component, node]
                earlier = stress
            before = modes
        image = following
    stacked = jnp.concatenate(moments + [jnp.zeros_like(moments[0])] * (8 - len(moments)), axis=0)
    total = jnp.broadcast_to(jnp.sum(stacked, axis=1, keepdims=True), (8, 128))
    chosen = lax.broadcasted_iota(jnp.int32, (8, 128), 0) == lax.broadcasted_iota(
        jnp.int32, (8, 128), 1
    )
    total = jnp.sum(jnp.where(chosen, total, 0.0), axis=0, keepdims=True)
    moment_ref[...] = jnp.broadcast_to(total, moment_ref.shape)


def sum_kernel(part_ref, total_ref):
    total = jnp.sum(part_ref[...], axis=0, keepdims=True)
    total_ref[...] = jnp.broadcast_to(total, total_ref.shape)


def dot_moments(moments, left, right, shift):
    total = 0.0
    for i, a in enumerate(left):
        for j, b in enumerate(right):
            total = total + a * b * moments[i + j + shift]
    return total


def coefficients(moments):
    zero = jnp.zeros_like(moments[0])
    solution = [zero] * ITERS
    residual = [zero + 1.0] + [zero] * ITERS
    direction = [zero + 1.0] + [zero] * (ITERS - 1)
    norm_now = moments[0]
    for step in range(ITERS):
        used = direction[: step + 1]
        image = dot_moments(moments, used, used, 0) + dot_moments(moments, used, used, 1)
        alpha = norm_now / image
        for k in range(step + 1):
            solution[k] = solution[k] + alpha * direction[k]
            residual[k] = residual[k] - alpha * direction[k]
        for k in range(step + 1):
            residual[k + 1] = residual[k + 1] - alpha * direction[k]
        if step + 1 < ITERS:
            used = residual[: step + 2]
            norm_next = dot_moments(moments, used, used, 0)
            beta = norm_next / norm_now
            for k in range(step + 2):
                direction[k] = residual[k] + beta * direction[k]
            norm_now = norm_next
    return solution, residual


def finish_kernel(image_ref, inverse_ref, part_ref, solution_ref, residual_ref):
    total = jnp.sum(part_ref[...], axis=0, keepdims=True)
    moments = [jnp.broadcast_to(total[:, k : k + 1], total.shape) for k in range(2 * ITERS)]
    along, left = coefficients(moments)
    depth = image_ref.shape[-1]
    reps = depth // total.shape[1]

    def spread(value):
        value = jnp.broadcast_to(value, (ROWS, value.shape[1]))
        return jnp.concatenate([value] * reps, axis=1)

    along = [spread(value) for value in along]
    left = [spread(value) for value in left]
    for component in range(3):
        for plane in range(PLANES):
            spot = component * PLANES + plane
            images = [image_ref[k, spot] for k in range(ITERS + 1)]
            value = sum(a * b for a, b in zip(along, images[:ITERS]))
            solution_ref[component, plane] = value * inverse_ref[plane]
            residual_ref[component, plane] = sum(a * b for a, b in zip(left, images))


def shaped(*shape):
    return jax.ShapeDtypeStruct(shape, jnp.float32)


def neighbours(axis, low_part, high_part):
    count = math.prod(lax.axis_size(name) for name in axis)
    forward = [(i, i + 1) for i in range(count - 1)]
    backward = [(target, source) for source, target in forward]
    return lax.ppermute(high_part, axis, forward), lax.ppermute(low_part, axis, backward)


def members(axes):
    return math.prod(lax.axis_size(name) for name in axes)


def exchanged(rows, axes):
    return lax.all_to_all(rows, axes, 0, 0, tiled=True)


def call(kernel, outs, *args, **options):
    return pl.pallas_call(
        kernel,
        out_shape=outs,
        compiler_params=pltpu.CompilerParams(vmem_limit_bytes=32 << 20),
        **options,
    )(*args)


def local(rhs_force, moduli, fixed_nodes, contact_nodes):
    depth = rhs_force.shape[3]
    count = (FIELDS + 1) * PLANES
    edge = shaped(count, EDGE, depth)
    arguments = (rhs_force, moduli, fixed_nodes, contact_nodes)
    arguments = [pltpu.with_memory_space_constraint(value, pltpu.HBM) for value in arguments]
    both, low, high = call(
        rows_kernel,
        (shaped(count, ROWS, depth), edge, edge),
        *arguments,
        in_specs=[pl.BlockSpec(memory_space=pltpu.HBM)] * len(arguments),
        scratch_shapes=[pltpu.VMEM(value.shape, value.dtype) for value in arguments]
        + [pltpu.SemaphoreType.DMA((len(arguments),))],
    )
    below, above = neighbours(("cross",), low, high)
    edge = shaped(FIELDS * DEEP + PLANES, TALL, depth)
    tall, low, high = call(
        planes_kernel, (shaped(count, TALL, depth), edge, edge), both, below, above
    )
    below, above = neighbours(DIG, low, high)
    image, inverse, moments = call(
        krylov_kernel,
        (
            shaped(ITERS + 1, 3 * PLANES, ROWS, depth),
            shaped(PLANES, ROWS, depth),
            shaped(members(SUM_FIRST), 128),
        ),
        tall,
        below,
        above,
    )
    moments = exchanged(moments, SUM_FIRST)
    moments = call(sum_kernel, shaped(members(SUM_LAST), 128), moments)
    moments = exchanged(moments, SUM_LAST)
    out = shaped(3, PLANES, ROWS, depth)
    return tuple(call(finish_kernel, (out, out), image, inverse, moments))


def solution(mesh):
    parts = DIG_SIZES + (mesh.shape["cross"],)
    split = jax.sharding.Mesh(mesh.devices.reshape(parts), DIG + ("cross",))
    return jax.shard_map(
        local,
        mesh=split,
        in_specs=(
            P(None, DIG, "cross", None),
            P(DIG, "cross", None),
            P(DIG, "cross", None),
            P(DIG, "cross", None),
        ),
        out_specs=(P(None, DIG, "cross", None), P(None, DIG, "cross", None)),
        check_vma=False,
    )
```

```python
import math

import jax
import jax.numpy as jnp
from jax import lax
from jax.experimental import pallas as pl
from jax.experimental.pallas import tpu as pltpu
from jax.sharding import PartitionSpec as P

ITERS = 3
POISSON = 0.3
PENALTY = 6.0
LAME_FIRST = POISSON / ((1.0 + POISSON) * (1.0 - 2.0 * POISSON))
SHEAR = 0.5 / (1.0 + POISSON)
ENTRY = (LAME_FIRST + 4.0 * SHEAR) / 9.0
RATIO = 2.0 * POISSON / (1.0 - 2.0 * POISSON)
DIG = ("x", "z", "core")
DIG_SIZES = (4, 12, 2)
SUM_FIRST = ("x", "cross")
SUM_LAST = ("z", "core")
PLANES = 4
ROWS = 8
EDGE = 4
DEEP = 3
FIELDS = 5
TALL = ROWS + 2 * EDGE


def up_z(value):
    depth = value.shape[1]
    lane = lax.broadcasted_iota(jnp.int32, value.shape, 1)
    return jnp.where(lane == depth - 1, 0.0, pltpu.roll(value, depth - 1, 1))


def down_z(value):
    lane = lax.broadcasted_iota(jnp.int32, value.shape, 1)
    return jnp.where(lane == 0, 0.0, pltpu.roll(value, 1, 1))


def up_y(value):
    return pltpu.roll(value, value.shape[0] - 1, 0)


def down_y(value):
    return pltpu.roll(value, 1, 0)


def node_modes(value):
    beyond = up_z(value)
    plus, minus = value + beyond, beyond - value
    plus_up, minus_up = up_y(plus), up_y(minus)
    return {
        "ss": plus + plus_up,
        "ds": plus_up - plus,
        "sd": minus + minus_up,
        "dd": minus_up - minus,
    }


def element_stress(low, high, weights):
    strain = []
    for component in range(3):
        modes = {}
        for name in ("ss", "ds", "sd", "dd"):
            modes["d" + name] = high[component][name] - low[component][name]
            if name != "ss":
                modes["s" + name] = high[component][name] + low[component][name]
        strain.append(modes)
    u, v, w = strain
    whole, third, ninth = weights
    trace = RATIO * (u["dss"] + v["sds"] + w["ssd"])
    xy = whole * (u["sds"] + v["dss"])
    xz = whole * (u["ssd"] + w["dss"])
    yz = whole * (v["ssd"] + w["sds"])

    def normal(value):
        return whole * (value + value + trace)

    def pair(one, other):
        half = 0.5 * (one + other)
        return whole * (one + half), whole * (other + half)

    u_dsd, v_sdd = pair(u["dsd"], v["sdd"])
    u_dds, w_sdd = pair(u["dds"], w["sdd"])
    v_dds, w_dsd = pair(v["dds"], w["dsd"])
    twist = u["sdd"] + v["dsd"] + w["dds"]
    return (
        {
            "dss": normal(u["dss"]),
            "sds": xy,
            "ssd": xz,
            "dsd": u_dsd,
            "dds": u_dds,
            "sdd": third * (twist + u["sdd"]),
            "ddd": ninth * u["ddd"],
        },
        {
            "sds": normal(v["sds"]),
            "dss": xy,
            "ssd": yz,
            "sdd": v_sdd,
            "dds": v_dds,
            "dsd": third * (twist + v["dsd"]),
            "ddd": ninth * v["ddd"],
        },
        {
            "ssd": normal(w["ssd"]),
            "dss": xz,
            "sds": yz,
            "sdd": w_sdd,
            "dsd": w_dsd,
            "dds": third * (twist + w["dds"]),
            "ddd": ninth * w["ddd"],
        },
    )


def node_force(low, high):
    total = {"ss": low["dss"] - high["dss"]}
    for name in ("ds", "sd", "dd"):
        total[name] = (low["s" + name] + low["d" + name]) + (high["s" + name] - high["d" + name])
    plus = (total["ss"] - total["ds"]) + down_y(total["ss"] + total["ds"])
    minus = (total["sd"] - total["dd"]) + down_y(total["sd"] + total["dd"])
    return (plus - minus) + down_z(plus + minus)


def rows_kernel(*refs):
    arguments, (both_ref, low_ref, high_ref) = refs[:4], refs[4:7]
    buffers, arrived = refs[7:11], refs[11]
    copies = [
        pltpu.make_async_copy(source, target, arrived.at[k])
        for k, (source, target) in enumerate(zip(arguments, buffers))
    ]
    for copy in copies:
        copy.start()
    for copy in copies:
        copy.wait()
    force_ref, moduli_ref, fixed_ref, contact_ref = buffers
    for plane in range(PLANES):
        free = 1.0 - fixed_ref[plane].astype(jnp.float32)
        contact = PENALTY * contact_ref[plane].astype(jnp.float32)
        packed = [free * force_ref[component, plane] for component in range(3)]
        packed += [free, contact, moduli_ref[plane]]
        for field, value in enumerate(packed):
            spot = field * PLANES + plane
            both_ref[spot] = value
            low_ref[spot] = value[:EDGE]
            high_ref[spot] = value[ROWS - EDGE :]


def planes_kernel(both_ref, below_ref, above_ref, tall_ref, inside_ref, outside_ref):
    first = lax.axis_index("core") == 0
    half = FIELDS * DEEP + PLANES
    for field in range(FIELDS + 1):
        tall = []
        for plane in range(PLANES):
            spot = field * PLANES + plane
            value = jnp.concatenate([below_ref[spot], both_ref[spot], above_ref[spot]], axis=0)
            tall_ref[spot] = value
            tall.append(value)
        deep = PLANES if field == FIELDS else DEEP
        for k in range(deep):
            low, high = tall[k], tall[PLANES - deep + k]
            spot = field * DEEP + k
            inside_ref[spot] = low
            inside_ref[half + spot] = high
            outside_ref[spot] = jnp.where(first, low, high)


def krylov_kernel(tall_ref, inside_ref, outside_ref, image_ref, inverse_ref, moment_ref):
    first = lax.axis_index("core") == 0
    half = FIELDS * DEEP + PLANES

    def plane_of(field, plane):
        deep = PLANES if field == FIELDS else DEEP
        if plane < 0:
            spot = field * DEEP + plane + deep
            return jnp.where(first, outside_ref[spot], inside_ref[spot])
        if plane >= PLANES:
            spot = field * DEEP + plane - PLANES
            return jnp.where(first, inside_ref[half + spot], outside_ref[spot])
        return tall_ref[field * PLANES + plane]

    def own(value):
        return value[EDGE : EDGE + ROWS]

    columns = {}
    for plane in range(-PLANES, 2 * PLANES):
        value = plane_of(FIELDS, plane)
        value = value + up_z(value)
        columns[plane] = value + up_y(value)
    whole = {
        plane: (0.125 * SHEAR / 16.0) * (columns[plane] + columns[plane + 1])
        for plane in range(-PLANES, 2 * PLANES - 1)
    }
    free, keep, inverse = {}, {}, {}
    image = {}
    for plane in range(-DEEP, PLANES + DEEP):
        free[plane] = plane_of(3, plane)
        keep[plane] = free[plane] * plane_of(4, plane) + (1.0 - free[plane])
        value = whole[plane - 1] + whole[plane]
        value = value + down_y(value)
        value = (ENTRY * 16.0 / SHEAR) * (value + down_z(value))
        inverse[plane] = 1.0 / (free[plane] * value + keep[plane])
        for component in range(3):
            image[component, plane] = plane_of(component, plane)
    row = lax.broadcasted_iota(jnp.int32, image[0, 0].shape, 0)
    mine = (row >= EDGE) & (row < EDGE + ROWS)
    moments = []

    def moment(left, right):
        total = 0.0
        for component in range(3):
            for plane in range(PLANES):
                total = total + left[component, plane] * right[component, plane]
        total = jnp.where(mine, total, 0.0)
        moments.append(jnp.sum(total, axis=0, keepdims=True))

    for plane in range(PLANES):
        inverse_ref[plane] = own(inverse[plane])
    for step in range(ITERS + 1):
        for component in range(3):
            for plane in range(PLANES):
                image_ref[step, component * PLANES + plane] = own(image[component, plane])
        if step:
            moment(vector, image)
        if step == ITERS:
            break
        reach = DEEP - step
        vector = {
            (component, plane): image[component, plane] * inverse[plane]
            for component in range(3)
            for plane in range(-reach, PLANES + reach)
        }
        moment(vector, image)
        following = {}
        for plane in range(-reach, PLANES + reach):
            modes = [node_modes(vector[component, plane]) for component in range(3)]
            if plane > -reach:
                scale = whole[plane - 1]
                stress = element_stress(
                    before, modes, (scale, scale * (1.0 / 3.0), scale * (5.5 / 9.0))
                )
                if plane > 1 - reach:
                    node = plane - 1
                    for component in range(3):
                        force = node_force(earlier[component], stress[component])
                        here = vector[component, node]
                        following[component, node] = (
                            free[node] * force + keep[node] * here
                        ) - image[component, node]
                earlier = stress
            before = modes
        image = following
    stacked = jnp.concatenate(moments + [jnp.zeros_like(moments[0])] * (8 - len(moments)), axis=0)
    total = jnp.broadcast_to(jnp.sum(stacked, axis=1, keepdims=True), (8, 128))
    chosen = lax.broadcasted_iota(jnp.int32, (8, 128), 0) == lax.broadcasted_iota(
        jnp.int32, (8, 128), 1
    )
    total = jnp.sum(jnp.where(chosen, total, 0.0), axis=0, keepdims=True)
    moment_ref[...] = jnp.broadcast_to(total, moment_ref.shape)


def sum_kernel(part_ref, total_ref):
    total = jnp.sum(part_ref[...], axis=0, keepdims=True)
    total_ref[...] = jnp.broadcast_to(total, total_ref.shape)


def dot_moments(moments, left, right, shift):
    total = 0.0
    for i, a in enumerate(left):
        for j, b in enumerate(right):
            total = total + a * b * moments[i + j + shift]
    return total


def coefficients(moments):
    zero = jnp.zeros_like(moments[0])
    solution = [zero] * ITERS
    residual = [zero + 1.0] + [zero] * ITERS
    direction = [zero + 1.0] + [zero] * (ITERS - 1)
    norm_now = moments[0]
    for step in range(ITERS):
        used = direction[: step + 1]
        image = dot_moments(moments, used, used, 0) + dot_moments(moments, used, used, 1)
        alpha = norm_now / image
        for k in range(step + 1):
            solution[k] = solution[k] + alpha * direction[k]
            residual[k] = residual[k] - alpha * direction[k]
        for k in range(step + 1):
            residual[k + 1] = residual[k + 1] - alpha * direction[k]
        if step + 1 < ITERS:
            used = residual[: step + 2]
            norm_next = dot_moments(moments, used, used, 0)
            beta = norm_next / norm_now
            for k in range(step + 2):
                direction[k] = residual[k] + beta * direction[k]
            norm_now = norm_next
    return solution, residual


def finish_kernel(image_ref, inverse_ref, part_ref, solution_ref, residual_ref):
    total = jnp.sum(part_ref[...], axis=0, keepdims=True)
    moments = [jnp.broadcast_to(total[:, k : k + 1], total.shape) for k in range(2 * ITERS)]
    along, left = coefficients(moments)
    depth = image_ref.shape[-1]
    reps = depth // total.shape[1]

    def spread(value):
        value = jnp.broadcast_to(value, (ROWS, value.shape[1]))
        return jnp.concatenate([value] * reps, axis=1)

    along = [spread(value) for value in along]
    left = [spread(value) for value in left]
    for component in range(3):
        for plane in range(PLANES):
            spot = component * PLANES + plane
            images = [image_ref[k, spot] for k in range(ITERS + 1)]
            value = sum(a * b for a, b in zip(along, images[:ITERS]))
            solution_ref[component, plane] = value * inverse_ref[plane]
            residual_ref[component, plane] = sum(a * b for a, b in zip(left, images))


def shaped(*shape):
    return jax.ShapeDtypeStruct(shape, jnp.float32)


def row_neighbours(low_part, high_part):
    count = lax.axis_size("cross")
    forward = [(i, i + 1) for i in range(count - 1)]
    backward = [(target, source) for source, target in forward]
    return lax.ppermute(high_part, "cross", forward), lax.ppermute(low_part, "cross", backward)


def next_chip(part):
    pairs = [(i, i + 1) for i in range(1, members(DIG) - 1, 2)]
    return lax.ppermute(part, DIG, pairs + [(target, source) for source, target in pairs])


def members(axes):
    return math.prod(lax.axis_size(name) for name in axes)


def exchanged(rows, axes):
    return lax.all_to_all(rows, axes, 0, 0, tiled=True)


def call(kernel, outs, *args, **options):
    return pl.pallas_call(
        kernel,
        out_shape=outs,
        compiler_params=pltpu.CompilerParams(vmem_limit_bytes=32 << 20),
        **options,
    )(*args)


def local(rhs_force, moduli, fixed_nodes, contact_nodes):
    depth = rhs_force.shape[3]
    count = (FIELDS + 1) * PLANES
    edge = shaped(count, EDGE, depth)
    arguments = (rhs_force, moduli, fixed_nodes, contact_nodes)
    arguments = [pltpu.with_memory_space_constraint(value, pltpu.HBM) for value in arguments]
    both, low, high = call(
        rows_kernel,
        (shaped(count, ROWS, depth), edge, edge),
        *arguments,
        in_specs=[pl.BlockSpec(memory_space=pltpu.HBM)] * len(arguments),
        scratch_shapes=[pltpu.VMEM(value.shape, value.dtype) for value in arguments]
        + [pltpu.SemaphoreType.DMA((len(arguments),))],
    )
    below, above = row_neighbours(low, high)
    half = FIELDS * DEEP + PLANES
    tall, inside, outside = call(
        planes_kernel,
        (shaped(count, TALL, depth), shaped(2 * half, TALL, depth), shaped(half, TALL, depth)),
        both,
        below,
        above,
    )
    outside = next_chip(outside)
    inside = exchanged(inside, ("core",))
    image, inverse, moments = call(
        krylov_kernel,
        (
            shaped(ITERS + 1, 3 * PLANES, ROWS, depth),
            shaped(PLANES, ROWS, depth),
            shaped(members(SUM_FIRST), 128),
        ),
        tall,
        inside,
        outside,
    )
    moments = exchanged(moments, SUM_FIRST)
    moments = call(sum_kernel, shaped(members(SUM_LAST), 128), moments)
    moments = exchanged(moments, SUM_LAST)
    out = shaped(3, PLANES, ROWS, depth)
    return tuple(call(finish_kernel, (out, out), image, inverse, moments))


def solution(mesh):
    parts = DIG_SIZES + (mesh.shape["cross"],)
    split = jax.sharding.Mesh(mesh.devices.reshape(parts), DIG + ("cross",))
    return jax.shard_map(
        local,
        mesh=split,
        in_specs=(
            P(None, DIG, "cross", None),
            P(DIG, "cross", None),
            P(DIG, "cross", None),
            P(DIG, "cross", None),
        ),
        out_specs=(P(None, DIG, "cross", None), P(None, DIG, "cross", None)),
        check_vma=False,
    )
```

```python
import math

import jax
import jax.numpy as jnp
from jax import lax
from jax.experimental import pallas as pl
from jax.experimental.pallas import tpu as pltpu
from jax.sharding import PartitionSpec as P

ITERS = 3
POISSON = 0.3
PENALTY = 6.0
LAME_FIRST = POISSON / ((1.0 + POISSON) * (1.0 - 2.0 * POISSON))
SHEAR = 0.5 / (1.0 + POISSON)
ENTRY = (LAME_FIRST + 4.0 * SHEAR) / 9.0
RATIO = 2.0 * POISSON / (1.0 - 2.0 * POISSON)
DIG = ("x", "z", "core")
DIG_SIZES = (4, 12, 2)
SUM_FIRST = ("x", "core", "cross")
SUM_LAST = ("z",)
PLANES = 4
ROWS = 8
EDGE = 4
DEEP = 3
FIELDS = 5
TALL = ROWS + 2 * EDGE


LANES = 128


def tiles(value):
    return [value[:, k : k + LANES] for k in range(0, value.shape[1], LANES)]


def up_z(value):
    lane = lax.broadcasted_iota(jnp.int32, (value.shape[0], LANES), 1)
    turned = [pltpu.roll(tile, LANES - 1, 1) for tile in tiles(value)] + [0.0]
    shifted = [
        jnp.where(lane == LANES - 1, after, here) for here, after in zip(turned, turned[1:])
    ]
    return jnp.concatenate(shifted, axis=1)


def down_z(value):
    lane = lax.broadcasted_iota(jnp.int32, (value.shape[0], LANES), 1)
    turned = [0.0] + [pltpu.roll(tile, 1, 1) for tile in tiles(value)]
    shifted = [jnp.where(lane == 0, before, here) for before, here in zip(turned, turned[1:])]
    return jnp.concatenate(shifted, axis=1)


def up_y(value):
    return pltpu.roll(value, value.shape[0] - 1, 0)


def down_y(value):
    return pltpu.roll(value, 1, 0)


def node_modes(value):
    beyond = up_z(value)
    plus, minus = value + beyond, beyond - value
    plus_up, minus_up = up_y(plus), up_y(minus)
    return {
        "ss": plus + plus_up,
        "ds": plus_up - plus,
        "sd": minus + minus_up,
        "dd": minus_up - minus,
    }


def element_stress(low, high, weights):
    strain = []
    for component in range(3):
        modes = {}
        for name in ("ss", "ds", "sd", "dd"):
            modes["d" + name] = high[component][name] - low[component][name]
            if name != "ss":
                modes["s" + name] = high[component][name] + low[component][name]
        strain.append(modes)
    u, v, w = strain
    whole, third, ninth = weights
    trace = RATIO * (u["dss"] + v["sds"] + w["ssd"])
    xy = whole * (u["sds"] + v["dss"])
    xz = whole * (u["ssd"] + w["dss"])
    yz = whole * (v["ssd"] + w["sds"])

    def normal(value):
        return whole * (value + value + trace)

    def pair(one, other):
        half = 0.5 * (one + other)
        return whole * (one + half), whole * (other + half)

    u_dsd, v_sdd = pair(u["dsd"], v["sdd"])
    u_dds, w_sdd = pair(u["dds"], w["sdd"])
    v_dds, w_dsd = pair(v["dds"], w["dsd"])
    twist = u["sdd"] + v["dsd"] + w["dds"]
    return (
        {
            "dss": normal(u["dss"]),
            "sds": xy,
            "ssd": xz,
            "dsd": u_dsd,
            "dds": u_dds,
            "sdd": third * (twist + u["sdd"]),
            "ddd": ninth * u["ddd"],
        },
        {
            "sds": normal(v["sds"]),
            "dss": xy,
            "ssd": yz,
            "sdd": v_sdd,
            "dds": v_dds,
            "dsd": third * (twist + v["dsd"]),
            "ddd": ninth * v["ddd"],
        },
        {
            "ssd": normal(w["ssd"]),
            "dss": xz,
            "sds": yz,
            "sdd": w_sdd,
            "dsd": w_dsd,
            "dds": third * (twist + w["dds"]),
            "ddd": ninth * w["ddd"],
        },
    )


def node_force(low, high):
    total = {"ss": low["dss"] - high["dss"]}
    for name in ("ds", "sd", "dd"):
        total[name] = (low["s" + name] + low["d" + name]) + (high["s" + name] - high["d" + name])
    plus = (total["ss"] - total["ds"]) + down_y(total["ss"] + total["ds"])
    minus = (total["sd"] - total["dd"]) + down_y(total["sd"] + total["dd"])
    return plus - minus, plus + minus


def rows_kernel(*refs):
    arguments, (both_ref, low_ref, high_ref) = refs[:4], refs[4:7]
    buffers, arrived = refs[7:11], refs[11]
    copies = [
        pltpu.make_async_copy(source, target, arrived.at[k])
        for k, (source, target) in enumerate(zip(arguments, buffers))
    ]
    for copy in copies:
        copy.start()
    for copy in copies:
        copy.wait()
    force_ref, moduli_ref, fixed_ref, contact_ref = buffers
    for plane in range(PLANES):
        free = 1.0 - fixed_ref[plane].astype(jnp.float32)
        contact = PENALTY * contact_ref[plane].astype(jnp.float32)
        packed = [free * force_ref[component, plane] for component in range(3)]
        packed += [free, contact, moduli_ref[plane]]
        for field, value in enumerate(packed):
            spot = field * PLANES + plane
            both_ref[spot] = value
            low_ref[spot] = value[:EDGE]
            high_ref[spot] = value[ROWS - EDGE :]


def planes_kernel(both_ref, below_ref, above_ref, tall_ref, inside_ref, outside_ref):
    first = lax.axis_index("core") == 0
    half = FIELDS * DEEP + PLANES
    for field in range(FIELDS + 1):
        tall = []
        for plane in range(PLANES):
            spot = field * PLANES + plane
            value = jnp.concatenate([below_ref[spot], both_ref[spot], above_ref[spot]], axis=0)
            tall_ref[spot] = value
            tall.append(value)
        deep = PLANES if field == FIELDS else DEEP
        for k in range(deep):
            low, high = tall[k], tall[PLANES - deep + k]
            spot = field * DEEP + k
            inside_ref[spot] = low
            inside_ref[half + spot] = high
            outside_ref[spot] = jnp.where(first, low, high)


def krylov_kernel(tall_ref, inside_ref, outside_ref, image_ref, inverse_ref, moment_ref):
    first = lax.axis_index("core") == 0
    half = FIELDS * DEEP + PLANES

    def plane_of(field, plane):
        deep = PLANES if field == FIELDS else DEEP
        if plane < 0:
            spot = field * DEEP + plane + deep
            return jnp.where(first, outside_ref[spot], inside_ref[spot])
        if plane >= PLANES:
            spot = field * DEEP + plane - PLANES
            return jnp.where(first, inside_ref[half + spot], outside_ref[spot])
        return tall_ref[field * PLANES + plane]

    def own(value):
        return value[EDGE : EDGE + ROWS]

    columns = {}
    for plane in range(-PLANES, 2 * PLANES):
        value = plane_of(FIELDS, plane)
        value = value + up_z(value)
        columns[plane] = value + up_y(value)
    whole = {
        plane: (0.125 * SHEAR / 16.0) * (columns[plane] + columns[plane + 1])
        for plane in range(-PLANES, 2 * PLANES - 1)
    }
    free, keep, inverse = {}, {}, {}
    image = {}
    for plane in range(-DEEP, PLANES + DEEP):
        free[plane] = plane_of(3, plane)
        keep[plane] = free[plane] * plane_of(4, plane) + (1.0 - free[plane])
        value = whole[plane - 1] + whole[plane]
        value = value + down_y(value)
        value = (ENTRY * 16.0 / SHEAR) * (value + down_z(value))
        inverse[plane] = 1.0 / (free[plane] * value + keep[plane])
        for component in range(3):
            image[component, plane] = plane_of(component, plane)
    row = lax.broadcasted_iota(jnp.int32, image[0, 0].shape, 0)
    mine = (row >= EDGE) & (row < EDGE + ROWS)
    moments = []

    def moment(left, right):
        total = 0.0
        for component in range(3):
            for plane in range(PLANES):
                total = total + left[component, plane] * right[component, plane]
        total = jnp.where(mine, total, 0.0)
        moments.append(jnp.sum(total, axis=0, keepdims=True))

    for plane in range(PLANES):
        inverse_ref[plane] = own(inverse[plane])
    for step in range(ITERS + 1):
        for component in range(3):
            for plane in range(PLANES):
                image_ref[step, component * PLANES + plane] = own(image[component, plane])
        if step:
            moment(vector, image)
        if step == ITERS:
            break
        reach = DEEP - step
        vector = {
            (component, plane): image[component, plane] * inverse[plane]
            for component in range(3)
            for plane in range(-reach, PLANES + reach)
        }
        moment(vector, image)
        following = {}
        for plane in range(-reach, PLANES + reach):
            full = [node_modes(vector[component, plane]) for component in range(3)]
            modes = [
                [{name: tiles(value)[k] for name, value in part.items()} for part in full]
                for k in range(full[0]["ss"].shape[1] // LANES)
            ]
            if plane > -reach:
                stress = []
                for low, high, scale in zip(before, modes, tiles(whole[plane - 1])):
                    stress.append(
                        element_stress(low, high, (scale, scale * (1.0 / 3.0), scale * (5.5 / 9.0)))
                    )
                if plane > 1 - reach:
                    node = plane - 1
                    for component in range(3):
                        ends = [
                            node_force(low[component], high[component])
                            for low, high in zip(earlier, stress)
                        ]
                        lower, upper = (jnp.concatenate(end, axis=1) for end in zip(*ends))
                        force = lower + down_z(upper)
                        here = vector[component, node]
                        following[component, node] = (
                            free[node] * force + keep[node] * here
                        ) - image[component, node]
                earlier = stress
            before = modes
        image = following
    stacked = jnp.concatenate(moments + [jnp.zeros_like(moments[0])] * (8 - len(moments)), axis=0)
    total = jnp.broadcast_to(jnp.sum(stacked, axis=1, keepdims=True), (8, 128))
    chosen = lax.broadcasted_iota(jnp.int32, (8, 128), 0) == lax.broadcasted_iota(
        jnp.int32, (8, 128), 1
    )
    total = jnp.sum(jnp.where(chosen, total, 0.0), axis=0, keepdims=True)
    moment_ref[...] = jnp.broadcast_to(total, moment_ref.shape)


def sum_kernel(part_ref, total_ref):
    total = jnp.sum(part_ref[...], axis=0, keepdims=True)
    total_ref[...] = jnp.broadcast_to(total, total_ref.shape)


def dot_moments(moments, left, right, shift):
    total = 0.0
    for i, a in enumerate(left):
        for j, b in enumerate(right):
            total = total + a * b * moments[i + j + shift]
    return total


def coefficients(moments):
    zero = jnp.zeros_like(moments[0])
    solution = [zero] * ITERS
    residual = [zero + 1.0] + [zero] * ITERS
    direction = [zero + 1.0] + [zero] * (ITERS - 1)
    norm_now = moments[0]
    for step in range(ITERS):
        used = direction[: step + 1]
        image = dot_moments(moments, used, used, 0) + dot_moments(moments, used, used, 1)
        alpha = norm_now / image
        for k in range(step + 1):
            solution[k] = solution[k] + alpha * direction[k]
            residual[k] = residual[k] - alpha * direction[k]
        for k in range(step + 1):
            residual[k + 1] = residual[k + 1] - alpha * direction[k]
        if step + 1 < ITERS:
            used = residual[: step + 2]
            norm_next = dot_moments(moments, used, used, 0)
            beta = norm_next / norm_now
            for k in range(step + 2):
                direction[k] = residual[k] + beta * direction[k]
            norm_now = norm_next
    return solution, residual


def finish_kernel(image_ref, inverse_ref, part_ref, solution_ref, residual_ref):
    total = jnp.sum(part_ref[...], axis=0, keepdims=True)
    moments = [jnp.broadcast_to(total[:, k : k + 1], total.shape) for k in range(2 * ITERS)]
    along, left = coefficients(moments)
    depth = image_ref.shape[-1]
    reps = depth // total.shape[1]

    def spread(value):
        value = jnp.broadcast_to(value, (ROWS, value.shape[1]))
        return jnp.concatenate([value] * reps, axis=1)

    along = [spread(value) for value in along]
    left = [spread(value) for value in left]
    for component in range(3):
        for plane in range(PLANES):
            spot = component * PLANES + plane
            images = [image_ref[k, spot] for k in range(ITERS + 1)]
            value = sum(a * b for a, b in zip(along, images[:ITERS]))
            solution_ref[component, plane] = value * inverse_ref[plane]
            residual_ref[component, plane] = sum(a * b for a, b in zip(left, images))


def shaped(*shape):
    return jax.ShapeDtypeStruct(shape, jnp.float32)


def row_neighbours(low_part, high_part):
    count = lax.axis_size("cross")
    forward = [(i, i + 1) for i in range(count - 1)]
    backward = [(target, source) for source, target in forward]
    return lax.ppermute(high_part, "cross", forward), lax.ppermute(low_part, "cross", backward)


def next_chip(part):
    pairs = [(i, i + 1) for i in range(1, members(DIG) - 1, 2)]
    return lax.ppermute(part, DIG, pairs + [(target, source) for source, target in pairs])


def members(axes):
    return math.prod(lax.axis_size(name) for name in axes)


def exchanged(rows, axes):
    return lax.all_to_all(rows, axes, 0, 0, tiled=True)


def call(kernel, outs, *args, **options):
    return pl.pallas_call(
        kernel,
        out_shape=outs,
        compiler_params=pltpu.CompilerParams(vmem_limit_bytes=32 << 20),
        **options,
    )(*args)


def local(rhs_force, moduli, fixed_nodes, contact_nodes):
    depth = rhs_force.shape[3]
    count = (FIELDS + 1) * PLANES
    edge = shaped(count, EDGE, depth)
    arguments = (rhs_force, moduli, fixed_nodes, contact_nodes)
    arguments = [pltpu.with_memory_space_constraint(value, pltpu.HBM) for value in arguments]
    both, low, high = call(
        rows_kernel,
        (shaped(count, ROWS, depth), edge, edge),
        *arguments,
        in_specs=[pl.BlockSpec(memory_space=pltpu.HBM)] * len(arguments),
        scratch_shapes=[pltpu.VMEM(value.shape, value.dtype) for value in arguments]
        + [pltpu.SemaphoreType.DMA((len(arguments),))],
    )
    below, above = row_neighbours(low, high)
    half = FIELDS * DEEP + PLANES
    tall, inside, outside = call(
        planes_kernel,
        (shaped(count, TALL, depth), shaped(2 * half, TALL, depth), shaped(half, TALL, depth)),
        both,
        below,
        above,
    )
    outside = next_chip(outside)
    inside = exchanged(inside, ("core",))
    image, inverse, moments = call(
        krylov_kernel,
        (
            shaped(ITERS + 1, 3 * PLANES, ROWS, depth),
            shaped(PLANES, ROWS, depth),
            shaped(members(SUM_FIRST), 128),
        ),
        tall,
        inside,
        outside,
    )
    moments = exchanged(moments, SUM_FIRST)
    moments = call(sum_kernel, shaped(members(SUM_LAST), 128), moments)
    moments = exchanged(moments, SUM_LAST)
    out = shaped(3, PLANES, ROWS, depth)
    return tuple(call(finish_kernel, (out, out), image, inverse, moments))


def solution(mesh):
    parts = DIG_SIZES + (mesh.shape["cross"],)
    split = jax.sharding.Mesh(mesh.devices.reshape(parts), DIG + ("cross",))
    return jax.shard_map(
        local,
        mesh=split,
        in_specs=(
            P(None, DIG, "cross", None),
            P(DIG, "cross", None),
            P(DIG, "cross", None),
            P(DIG, "cross", None),
        ),
        out_specs=(P(None, DIG, "cross", None), P(None, DIG, "cross", None)),
        check_vma=False,
    )
```

```python
import math

import jax
import jax.numpy as jnp
from jax import lax
from jax.experimental import pallas as pl
from jax.experimental.pallas import tpu as pltpu
from jax.sharding import PartitionSpec as P

ITERS = 3
POISSON = 0.3
PENALTY = 6.0
LAME_FIRST = POISSON / ((1.0 + POISSON) * (1.0 - 2.0 * POISSON))
SHEAR = 0.5 / (1.0 + POISSON)
ENTRY = (LAME_FIRST + 4.0 * SHEAR) / 9.0
RATIO = 2.0 * POISSON / (1.0 - 2.0 * POISSON)
DIG = ("x", "z", "core")
DIG_SIZES = (4, 12, 2)
SUM_FIRST = ("x", "core", "cross")
SUM_LAST = ("z",)
PLANES = 4
ROWS = 8
EDGE = 4
DEEP = 3
FIELDS = 5
TALL = ROWS + 2 * EDGE
HALF = FIELDS * (DEEP - 1) + DEEP + 3


LANES = 128


def tiles(value):
    return [value[:, k : k + LANES] for k in range(0, value.shape[1], LANES)]


def up_z(value):
    lane = lax.broadcasted_iota(jnp.int32, (value.shape[0], LANES), 1)
    turned = [pltpu.roll(tile, LANES - 1, 1) for tile in tiles(value)] + [0.0]
    shifted = [
        jnp.where(lane == LANES - 1, after, here) for here, after in zip(turned, turned[1:])
    ]
    return jnp.concatenate(shifted, axis=1)


def down_z(value):
    lane = lax.broadcasted_iota(jnp.int32, (value.shape[0], LANES), 1)
    turned = [0.0] + [pltpu.roll(tile, 1, 1) for tile in tiles(value)]
    shifted = [jnp.where(lane == 0, before, here) for before, here in zip(turned, turned[1:])]
    return jnp.concatenate(shifted, axis=1)


def up_y(value):
    return pltpu.roll(value, value.shape[0] - 1, 0)


def down_y(value):
    return pltpu.roll(value, 1, 0)


def node_modes(value):
    beyond = up_z(value)
    plus, minus = value + beyond, beyond - value
    plus_up, minus_up = up_y(plus), up_y(minus)
    return {
        "ss": plus + plus_up,
        "ds": plus_up - plus,
        "sd": minus + minus_up,
        "dd": minus_up - minus,
    }


def element_stress(low, high, weights):
    strain = []
    for component in range(3):
        modes = {}
        for name in ("ss", "ds", "sd", "dd"):
            modes["d" + name] = high[component][name] - low[component][name]
            if name != "ss":
                modes["s" + name] = high[component][name] + low[component][name]
        strain.append(modes)
    u, v, w = strain
    whole, third, ninth = weights
    trace = RATIO * (u["dss"] + v["sds"] + w["ssd"])
    xy = whole * (u["sds"] + v["dss"])
    xz = whole * (u["ssd"] + w["dss"])
    yz = whole * (v["ssd"] + w["sds"])

    def normal(value):
        return whole * (value + value + trace)

    def pair(one, other):
        half = 0.5 * (one + other)
        return whole * (one + half), whole * (other + half)

    u_dsd, v_sdd = pair(u["dsd"], v["sdd"])
    u_dds, w_sdd = pair(u["dds"], w["sdd"])
    v_dds, w_dsd = pair(v["dds"], w["dsd"])
    twist = u["sdd"] + v["dsd"] + w["dds"]
    return (
        {
            "dss": normal(u["dss"]),
            "sds": xy,
            "ssd": xz,
            "dsd": u_dsd,
            "dds": u_dds,
            "sdd": third * (twist + u["sdd"]),
            "ddd": ninth * u["ddd"],
        },
        {
            "sds": normal(v["sds"]),
            "dss": xy,
            "ssd": yz,
            "sdd": v_sdd,
            "dds": v_dds,
            "dsd": third * (twist + v["dsd"]),
            "ddd": ninth * v["ddd"],
        },
        {
            "ssd": normal(w["ssd"]),
            "dss": xz,
            "sds": yz,
            "sdd": w_sdd,
            "dsd": w_dsd,
            "dds": third * (twist + w["dds"]),
            "ddd": ninth * w["ddd"],
        },
    )


def node_force(low, high):
    total = {"ss": low["dss"] - high["dss"]}
    for name in ("ds", "sd", "dd"):
        total[name] = (low["s" + name] + low["d" + name]) + (high["s" + name] - high["d" + name])
    plus = (total["ss"] - total["ds"]) + down_y(total["ss"] + total["ds"])
    minus = (total["sd"] - total["dd"]) + down_y(total["sd"] + total["dd"])
    return plus - minus, plus + minus


def rows_kernel(*refs):
    arguments, (both_ref, low_ref, high_ref) = refs[:4], refs[4:7]
    buffers, arrived = refs[7:11], refs[11]
    copies = [
        pltpu.make_async_copy(source, target, arrived.at[k])
        for k, (source, target) in enumerate(zip(arguments, buffers))
    ]
    for copy in copies:
        copy.start()
    for copy in copies:
        copy.wait()
    force_ref, moduli_ref, fixed_ref, contact_ref = buffers
    for plane in range(PLANES):
        free = 1.0 - fixed_ref[plane].astype(jnp.float32)
        contact = PENALTY * contact_ref[plane].astype(jnp.float32)
        packed = [free * force_ref[component, plane] for component in range(3)]
        packed += [free, contact, moduli_ref[plane]]
        for field, value in enumerate(packed):
            spot = field * PLANES + plane
            both_ref[spot] = value
            low_ref[spot] = value[:EDGE]
            high_ref[spot] = value[ROWS - EDGE :]


def column(moduli):
    value = moduli + up_z(moduli)
    return value + up_y(value)


def scaled_modulus(lower, upper):
    return (0.125 * SHEAR / 16.0) * (lower + upper)


def inverse_diagonal(below, above, free, keep):
    value = below + above
    value = value + down_y(value)
    value = (ENTRY * 16.0 / SHEAR) * (value + down_z(value))
    return 1.0 / (free * value + keep)


def kept(free, contact):
    return free * contact + (1.0 - free)


def edge_spot(field, ring):
    if field < FIELDS and ring == DEEP:
        return HALF - 3 + field
    return field * (DEEP - 1) + ring - 1


def planes_kernel(both_ref, below_ref, above_ref, tall_ref, inside_ref, outside_ref):
    first = lax.axis_index("core") == 0
    tall = {}
    for field in range(FIELDS + 1):
        for plane in range(PLANES):
            spot = field * PLANES + plane
            value = jnp.concatenate([below_ref[spot], both_ref[spot], above_ref[spot]], axis=0)
            tall_ref[spot] = value
            tall[field, plane] = value

    def pack(field, ring, low, high):
        spot = edge_spot(field, ring)
        inside_ref[spot] = low
        inside_ref[HALF + spot] = high
        outside_ref[spot] = jnp.where(first, low, high)

    for field in range(FIELDS + 1):
        for ring in range(1, DEEP + 1 if field == FIELDS else DEEP):
            pack(field, ring, tall[field, ring - 1], tall[field, PLANES - ring])
    columns = [column(tall[FIELDS, plane]) for plane in range(PLANES)]
    whole = [scaled_modulus(lower, upper) for lower, upper in zip(columns, columns[1:])]
    ends = []
    for plane in (DEEP - 1, PLANES - DEEP):
        free = tall[3, plane]
        inverse = inverse_diagonal(
            whole[plane - 1], whole[plane], free, kept(free, tall[4, plane])
        )
        ends.append([tall[component, plane] * inverse for component in range(3)])
    for component, (low, high) in enumerate(zip(*ends)):
        pack(component, DEEP, low, high)


def krylov_kernel(tall_ref, inside_ref, outside_ref, image_ref, inverse_ref, moment_ref):
    first = lax.axis_index("core") == 0

    def plane_of(field, plane):
        if plane < 0:
            spot = edge_spot(field, -plane)
            return jnp.where(first, outside_ref[spot], inside_ref[spot])
        if plane >= PLANES:
            spot = edge_spot(field, plane - PLANES + 1)
            return jnp.where(first, inside_ref[HALF + spot], outside_ref[spot])
        return tall_ref[field * PLANES + plane]

    def own(value):
        return value[EDGE : EDGE + ROWS]

    columns = {plane: column(plane_of(FIELDS, plane)) for plane in range(-DEEP, PLANES + DEEP)}
    whole = {
        plane: scaled_modulus(columns[plane], columns[plane + 1])
        for plane in range(-DEEP, PLANES + DEEP - 1)
    }
    free, keep, inverse = {}, {}, {}
    image = {}
    for plane in range(1 - DEEP, PLANES + DEEP - 1):
        free[plane] = plane_of(3, plane)
        keep[plane] = kept(free[plane], plane_of(4, plane))
        inverse[plane] = inverse_diagonal(whole[plane - 1], whole[plane], free[plane], keep[plane])
        for component in range(3):
            image[component, plane] = plane_of(component, plane)
    row = lax.broadcasted_iota(jnp.int32, image[0, 0].shape, 0)
    mine = (row >= EDGE) & (row < EDGE + ROWS)
    moments = []

    def moment(left, right):
        total = 0.0
        for component in range(3):
            for plane in range(PLANES):
                total = total + left[component, plane] * right[component, plane]
        total = jnp.where(mine, total, 0.0)
        moments.append(jnp.sum(total, axis=0, keepdims=True))

    for plane in range(PLANES):
        inverse_ref[plane] = own(inverse[plane])
    for step in range(ITERS + 1):
        for component in range(3):
            for plane in range(PLANES):
                image_ref[step, component * PLANES + plane] = own(image[component, plane])
        if step:
            moment(vector, image)
        if step == ITERS:
            break
        reach = DEEP - step
        vector = {
            (component, plane): value * inverse[plane]
            for (component, plane), value in image.items()
        }
        if reach == DEEP:
            for component in range(3):
                for plane in (-DEEP, PLANES + DEEP - 1):
                    vector[component, plane] = plane_of(component, plane)
        moment(vector, image)
        following = {}
        for plane in range(-reach, PLANES + reach):
            full = [node_modes(vector[component, plane]) for component in range(3)]
            modes = [
                [{name: tiles(value)[k] for name, value in part.items()} for part in full]
                for k in range(full[0]["ss"].shape[1] // LANES)
            ]
            if plane > -reach:
                stress = []
                for low, high, scale in zip(before, modes, tiles(whole[plane - 1])):
                    stress.append(
                        element_stress(low, high, (scale, scale * (1.0 / 3.0), scale * (5.5 / 9.0)))
                    )
                if plane > 1 - reach:
                    node = plane - 1
                    for component in range(3):
                        ends = [
                            node_force(low[component], high[component])
                            for low, high in zip(earlier, stress)
                        ]
                        lower, upper = (jnp.concatenate(end, axis=1) for end in zip(*ends))
                        force = lower + down_z(upper)
                        here = vector[component, node]
                        following[component, node] = (
                            free[node] * force + keep[node] * here
                        ) - image[component, node]
                earlier = stress
            before = modes
        image = following
    stacked = jnp.concatenate(moments + [jnp.zeros_like(moments[0])] * (8 - len(moments)), axis=0)
    total = jnp.broadcast_to(jnp.sum(stacked, axis=1, keepdims=True), (8, 128))
    chosen = lax.broadcasted_iota(jnp.int32, (8, 128), 0) == lax.broadcasted_iota(
        jnp.int32, (8, 128), 1
    )
    total = jnp.sum(jnp.where(chosen, total, 0.0), axis=0, keepdims=True)
    moment_ref[...] = jnp.broadcast_to(total, moment_ref.shape)


def sum_kernel(part_ref, total_ref):
    total = jnp.sum(part_ref[...], axis=0, keepdims=True)
    total_ref[...] = jnp.broadcast_to(total, total_ref.shape)


def dot_moments(moments, left, right, shift):
    total = 0.0
    for i, a in enumerate(left):
        for j, b in enumerate(right):
            total = total + a * b * moments[i + j + shift]
    return total


def coefficients(moments):
    zero = jnp.zeros_like(moments[0])
    solution = [zero] * ITERS
    residual = [zero + 1.0] + [zero] * ITERS
    direction = [zero + 1.0] + [zero] * (ITERS - 1)
    norm_now = moments[0]
    for step in range(ITERS):
        used = direction[: step + 1]
        image = dot_moments(moments, used, used, 0) + dot_moments(moments, used, used, 1)
        alpha = norm_now / image
        for k in range(step + 1):
            solution[k] = solution[k] + alpha * direction[k]
            residual[k] = residual[k] - alpha * direction[k]
        for k in range(step + 1):
            residual[k + 1] = residual[k + 1] - alpha * direction[k]
        if step + 1 < ITERS:
            used = residual[: step + 2]
            norm_next = dot_moments(moments, used, used, 0)
            beta = norm_next / norm_now
            for k in range(step + 2):
                direction[k] = residual[k] + beta * direction[k]
            norm_now = norm_next
    return solution, residual


def finish_kernel(image_ref, inverse_ref, part_ref, solution_ref, residual_ref):
    total = jnp.sum(part_ref[...], axis=0, keepdims=True)
    moments = [jnp.broadcast_to(total[:, k : k + 1], total.shape) for k in range(2 * ITERS)]
    along, left = coefficients(moments)
    depth = image_ref.shape[-1]
    reps = depth // total.shape[1]

    def spread(value):
        value = jnp.broadcast_to(value, (ROWS, value.shape[1]))
        return jnp.concatenate([value] * reps, axis=1)

    along = [spread(value) for value in along]
    left = [spread(value) for value in left]
    for component in range(3):
        for plane in range(PLANES):
            spot = component * PLANES + plane
            images = [image_ref[k, spot] for k in range(ITERS + 1)]
            value = sum(a * b for a, b in zip(along, images[:ITERS]))
            solution_ref[component, plane] = value * inverse_ref[plane]
            residual_ref[component, plane] = sum(a * b for a, b in zip(left, images))


def shaped(*shape):
    return jax.ShapeDtypeStruct(shape, jnp.float32)


def row_neighbours(low_part, high_part):
    count = lax.axis_size("cross")
    forward = [(i, i + 1) for i in range(count - 1)]
    backward = [(target, source) for source, target in forward]
    return lax.ppermute(high_part, "cross", forward), lax.ppermute(low_part, "cross", backward)


def next_chip(part):
    pairs = [(i, i + 1) for i in range(1, members(DIG) - 1, 2)]
    return lax.ppermute(part, DIG, pairs + [(target, source) for source, target in pairs])


def members(axes):
    return math.prod(lax.axis_size(name) for name in axes)


def exchanged(rows, axes):
    return lax.all_to_all(rows, axes, 0, 0, tiled=True)


def call(kernel, outs, *args, **options):
    return pl.pallas_call(
        kernel,
        out_shape=outs,
        compiler_params=pltpu.CompilerParams(vmem_limit_bytes=32 << 20),
        **options,
    )(*args)


def local(rhs_force, moduli, fixed_nodes, contact_nodes):
    depth = rhs_force.shape[3]
    count = (FIELDS + 1) * PLANES
    edge = shaped(count, EDGE, depth)
    arguments = (rhs_force, moduli, fixed_nodes, contact_nodes)
    arguments = [pltpu.with_memory_space_constraint(value, pltpu.HBM) for value in arguments]
    both, low, high = call(
        rows_kernel,
        (shaped(count, ROWS, depth), edge, edge),
        *arguments,
        in_specs=[pl.BlockSpec(memory_space=pltpu.HBM)] * len(arguments),
        scratch_shapes=[pltpu.VMEM(value.shape, value.dtype) for value in arguments]
        + [pltpu.SemaphoreType.DMA((len(arguments),))],
    )
    below, above = row_neighbours(low, high)
    tall, inside, outside = call(
        planes_kernel,
        (shaped(count, TALL, depth), shaped(2 * HALF, TALL, depth), shaped(HALF, TALL, depth)),
        both,
        below,
        above,
    )
    outside = next_chip(outside)
    inside = exchanged(inside, ("core",))
    image, inverse, moments = call(
        krylov_kernel,
        (
            shaped(ITERS + 1, 3 * PLANES, ROWS, depth),
            shaped(PLANES, ROWS, depth),
            shaped(members(SUM_FIRST), 128),
        ),
        tall,
        inside,
        outside,
    )
    moments = exchanged(moments, SUM_FIRST)
    moments = call(sum_kernel, shaped(members(SUM_LAST), 128), moments)
    moments = exchanged(moments, SUM_LAST)
    out = shaped(3, PLANES, ROWS, depth)
    return tuple(call(finish_kernel, (out, out), image, inverse, moments))


def solution(mesh):
    parts = DIG_SIZES + (mesh.shape["cross"],)
    split = jax.sharding.Mesh(mesh.devices.reshape(parts), DIG + ("cross",))
    return jax.shard_map(
        local,
        mesh=split,
        in_specs=(
            P(None, DIG, "cross", None),
            P(DIG, "cross", None),
            P(DIG, "cross", None),
            P(DIG, "cross", None),
        ),
        out_specs=(P(None, DIG, "cross", None), P(None, DIG, "cross", None)),
        check_vma=False,
    )
```

```python
import math

import jax
import jax.numpy as jnp
from jax import lax
from jax.experimental import pallas as pl
from jax.experimental.pallas import tpu as pltpu
from jax.sharding import PartitionSpec as P

ITERS = 3
POISSON = 0.3
PENALTY = 6.0
LAME_FIRST = POISSON / ((1.0 + POISSON) * (1.0 - 2.0 * POISSON))
SHEAR = 0.5 / (1.0 + POISSON)
ENTRY = (LAME_FIRST + 4.0 * SHEAR) / 9.0
RATIO = 2.0 * POISSON / (1.0 - 2.0 * POISSON)
DIG = ("x", "z", "core")
DIG_SIZES = (4, 12, 2)
SUM_FIRST = ("x", "core", "cross")
SUM_LAST = ("z",)
PLANES = 4
ROWS = 8
EDGE = 4
DEEP = 3
FIELDS = 5
TALL = ROWS + 2 * EDGE
HALF = FIELDS * (DEEP - 1) + DEEP + 3


LANES = 128


def tiles(value):
    return [value[:, k : k + LANES] for k in range(0, value.shape[1], LANES)]


def up_z(value):
    lane = lax.broadcasted_iota(jnp.int32, (value.shape[0], LANES), 1)
    turned = [pltpu.roll(tile, LANES - 1, 1) for tile in tiles(value)] + [0.0]
    shifted = [
        jnp.where(lane == LANES - 1, after, here) for here, after in zip(turned, turned[1:])
    ]
    return jnp.concatenate(shifted, axis=1)


def down_z(value):
    lane = lax.broadcasted_iota(jnp.int32, (value.shape[0], LANES), 1)
    turned = [0.0] + [pltpu.roll(tile, 1, 1) for tile in tiles(value)]
    shifted = [jnp.where(lane == 0, before, here) for before, here in zip(turned, turned[1:])]
    return jnp.concatenate(shifted, axis=1)


def up_y(value):
    return pltpu.roll(value, value.shape[0] - 1, 0)


def down_y(value):
    return pltpu.roll(value, 1, 0)


def node_modes(value):
    beyond = up_z(value)
    plus, minus = value + beyond, beyond - value
    plus_up, minus_up = up_y(plus), up_y(minus)
    return {
        "ss": plus + plus_up,
        "ds": plus_up - plus,
        "sd": minus + minus_up,
        "dd": minus_up - minus,
    }


def element_stress(low, high, weights):
    strain = []
    for component in range(3):
        modes = {}
        for name in ("ss", "ds", "sd", "dd"):
            modes["d" + name] = high[component][name] - low[component][name]
            if name != "ss":
                modes["s" + name] = high[component][name] + low[component][name]
        strain.append(modes)
    u, v, w = strain
    whole, third, ninth = weights
    trace = RATIO * (u["dss"] + v["sds"] + w["ssd"])
    xy = whole * (u["sds"] + v["dss"])
    xz = whole * (u["ssd"] + w["dss"])
    yz = whole * (v["ssd"] + w["sds"])

    def normal(value):
        return whole * (value + value + trace)

    def pair(one, other):
        half = 0.5 * (one + other)
        return whole * (one + half), whole * (other + half)

    u_dsd, v_sdd = pair(u["dsd"], v["sdd"])
    u_dds, w_sdd = pair(u["dds"], w["sdd"])
    v_dds, w_dsd = pair(v["dds"], w["dsd"])
    twist = u["sdd"] + v["dsd"] + w["dds"]
    return (
        {
            "dss": normal(u["dss"]),
            "sds": xy,
            "ssd": xz,
            "dsd": u_dsd,
            "dds": u_dds,
            "sdd": third * (twist + u["sdd"]),
            "ddd": ninth * u["ddd"],
        },
        {
            "sds": normal(v["sds"]),
            "dss": xy,
            "ssd": yz,
            "sdd": v_sdd,
            "dds": v_dds,
            "dsd": third * (twist + v["dsd"]),
            "ddd": ninth * v["ddd"],
        },
        {
            "ssd": normal(w["ssd"]),
            "dss": xz,
            "sds": yz,
            "sdd": w_sdd,
            "dsd": w_dsd,
            "dds": third * (twist + w["dds"]),
            "ddd": ninth * w["ddd"],
        },
    )


def node_force(low, high):
    total = {"ss": low["dss"] - high["dss"]}
    for name in ("ds", "sd", "dd"):
        total[name] = (low["s" + name] + low["d" + name]) + (high["s" + name] - high["d" + name])
    plus = (total["ss"] - total["ds"]) + down_y(total["ss"] + total["ds"])
    minus = (total["sd"] - total["dd"]) + down_y(total["sd"] + total["dd"])
    return plus - minus, plus + minus


def rows_kernel(*refs):
    arguments, (both_ref, low_ref, high_ref) = refs[:4], refs[4:7]
    buffers, arrived = refs[7:11], refs[11]
    copies = [
        pltpu.make_async_copy(source, target, arrived.at[k])
        for k, (source, target) in enumerate(zip(arguments, buffers))
    ]
    for copy in copies:
        copy.start()
    for copy in copies:
        copy.wait()
    force_ref, moduli_ref, fixed_ref, contact_ref = buffers
    for plane in range(PLANES):
        free = 1.0 - fixed_ref[plane].astype(jnp.float32)
        contact = PENALTY * contact_ref[plane].astype(jnp.float32)
        packed = [free * force_ref[component, plane] for component in range(3)]
        packed += [free, contact, moduli_ref[plane]]
        for field, value in enumerate(packed):
            spot = field * PLANES + plane
            both_ref[spot] = value
            low_ref[spot] = value[:EDGE]
            high_ref[spot] = value[ROWS - EDGE :]


def column(moduli):
    value = moduli + up_z(moduli)
    return value + up_y(value)


def scaled_modulus(lower, upper):
    return (0.125 * SHEAR / 16.0) * (lower + upper)


def inverse_diagonal(below, above, free, keep):
    value = below + above
    value = value + down_y(value)
    value = (ENTRY * 16.0 / SHEAR) * (value + down_z(value))
    return 1.0 / (free * value + keep)


def kept(free, contact):
    return free * contact + (1.0 - free)


def edge_spot(field, ring):
    if field < FIELDS and ring == DEEP:
        return HALF - 3 + field
    return field * (DEEP - 1) + ring - 1


def planes_kernel(both_ref, below_ref, above_ref, tall_ref, inside_ref, outside_ref):
    first = lax.axis_index("core") == 0
    tall = {}
    for field in range(FIELDS + 1):
        for plane in range(PLANES):
            spot = field * PLANES + plane
            value = jnp.concatenate([below_ref[spot], both_ref[spot], above_ref[spot]], axis=0)
            tall_ref[spot] = value
            tall[field, plane] = value

    def pack(field, ring, low, high):
        spot = edge_spot(field, ring)
        inside_ref[spot] = low
        inside_ref[HALF + spot] = high
        outside_ref[spot] = jnp.where(first, low, high)

    for field in range(FIELDS + 1):
        for ring in range(1, DEEP + 1 if field == FIELDS else DEEP):
            pack(field, ring, tall[field, ring - 1], tall[field, PLANES - ring])
    columns = [column(tall[FIELDS, plane]) for plane in range(PLANES)]
    whole = [scaled_modulus(lower, upper) for lower, upper in zip(columns, columns[1:])]
    ends = []
    for plane in (DEEP - 1, PLANES - DEEP):
        free = tall[3, plane]
        inverse = inverse_diagonal(
            whole[plane - 1], whole[plane], free, kept(free, tall[4, plane])
        )
        ends.append([tall[component, plane] * inverse for component in range(3)])
    for component, (low, high) in enumerate(zip(*ends)):
        pack(component, DEEP, low, high)


def krylov_kernel(tall_ref, inside_ref, outside_ref, image_ref, inverse_ref, moment_ref):
    first = lax.axis_index("core") == 0

    def plane_of(field, plane):
        if plane < 0:
            spot = edge_spot(field, -plane)
            return jnp.where(first, outside_ref[spot], inside_ref[spot])
        if plane >= PLANES:
            spot = edge_spot(field, plane - PLANES + 1)
            return jnp.where(first, inside_ref[HALF + spot], outside_ref[spot])
        return tall_ref[field * PLANES + plane]

    def own(value):
        return value[EDGE : EDGE + ROWS]

    columns = {plane: column(plane_of(FIELDS, plane)) for plane in range(-DEEP, PLANES + DEEP)}
    whole = {
        plane: scaled_modulus(columns[plane], columns[plane + 1])
        for plane in range(-DEEP, PLANES + DEEP - 1)
    }
    free, keep, inverse = {}, {}, {}
    image = {}
    for plane in range(1 - DEEP, PLANES + DEEP - 1):
        free[plane] = plane_of(3, plane)
        keep[plane] = kept(free[plane], plane_of(4, plane))
        inverse[plane] = inverse_diagonal(whole[plane - 1], whole[plane], free[plane], keep[plane])
        for component in range(3):
            image[component, plane] = plane_of(component, plane)
    row = lax.broadcasted_iota(jnp.int32, image[0, 0].shape, 0)
    mine = (row >= EDGE) & (row < EDGE + ROWS)
    moments = []

    def moment(left, right):
        total = 0.0
        for component in range(3):
            for plane in range(PLANES):
                total = total + left[component, plane] * right[component, plane]
        total = jnp.where(mine, total, 0.0)
        moments.append(jnp.sum(total, axis=0, keepdims=True))

    for plane in range(PLANES):
        inverse_ref[plane] = own(inverse[plane])
    for step in range(ITERS + 1):
        for component in range(3):
            for plane in range(PLANES):
                image_ref[step, component * PLANES + plane] = own(image[component, plane])
        if step:
            moment(vector, image)
        if step == ITERS:
            break
        reach = DEEP - step
        vector = {
            (component, plane): value * inverse[plane]
            for (component, plane), value in image.items()
        }
        if reach == DEEP:
            for component in range(3):
                for plane in (-DEEP, PLANES + DEEP - 1):
                    vector[component, plane] = plane_of(component, plane)
        moment(vector, image)
        following = {}
        for plane in range(-reach, PLANES + reach):
            full = [node_modes(vector[component, plane]) for component in range(3)]
            modes = [
                [{name: tiles(value)[k] for name, value in part.items()} for part in full]
                for k in range(full[0]["ss"].shape[1] // LANES)
            ]
            if plane > -reach:
                stress = []
                for low, high, scale in zip(before, modes, tiles(whole[plane - 1])):
                    stress.append(
                        element_stress(low, high, (scale, scale * (1.0 / 3.0), scale * (5.5 / 9.0)))
                    )
                if plane > 1 - reach:
                    node = plane - 1
                    for component in range(3):
                        ends = [
                            node_force(low[component], high[component])
                            for low, high in zip(earlier, stress)
                        ]
                        lower, upper = (jnp.concatenate(end, axis=1) for end in zip(*ends))
                        force = lower + down_z(upper)
                        here = vector[component, node]
                        following[component, node] = (
                            free[node] * force + keep[node] * here
                        ) - image[component, node]
                earlier = stress
            before = modes
        image = following
    stacked = jnp.concatenate(moments + [jnp.zeros_like(moments[0])] * (8 - len(moments)), axis=0)
    total = jnp.broadcast_to(jnp.sum(stacked, axis=1, keepdims=True), (8, 128))
    chosen = lax.broadcasted_iota(jnp.int32, (8, 128), 0) == lax.broadcasted_iota(
        jnp.int32, (8, 128), 1
    )
    total = jnp.sum(jnp.where(chosen, total, 0.0), axis=0, keepdims=True)
    moment_ref[...] = jnp.broadcast_to(total, moment_ref.shape)


def sum_kernel(part_ref, total_ref):
    total = jnp.sum(part_ref[...], axis=0, keepdims=True)
    total_ref[...] = jnp.broadcast_to(total, total_ref.shape)


def dot_moments(moments, left, right, shift):
    total = 0.0
    for i, a in enumerate(left):
        for j, b in enumerate(right):
            total = total + a * b * moments[i + j + shift]
    return total


def coefficients(moments):
    zero = jnp.zeros_like(moments[0])
    solution = [zero] * ITERS
    residual = [zero + 1.0] + [zero] * ITERS
    direction = [zero + 1.0] + [zero] * (ITERS - 1)
    norm_now = moments[0]
    for step in range(ITERS):
        used = direction[: step + 1]
        image = dot_moments(moments, used, used, 0) + dot_moments(moments, used, used, 1)
        alpha = norm_now / image
        for k in range(step + 1):
            solution[k] = solution[k] + alpha * direction[k]
            residual[k] = residual[k] - alpha * direction[k]
        for k in range(step + 1):
            residual[k + 1] = residual[k + 1] - alpha * direction[k]
        if step + 1 < ITERS:
            used = residual[: step + 2]
            norm_next = dot_moments(moments, used, used, 0)
            beta = norm_next / norm_now
            for k in range(step + 2):
                direction[k] = residual[k] + beta * direction[k]
            norm_now = norm_next
    return solution, residual


def finish_kernel(
    image_ref, inverse_ref, part_ref, solution_out, residual_out, solution_ref, residual_ref, sent
):
    total = jnp.sum(part_ref[...], axis=0, keepdims=True)
    moments = [jnp.broadcast_to(total[:, k : k + 1], total.shape) for k in range(2 * ITERS)]
    along, left = coefficients(moments)
    depth = image_ref.shape[-1]
    reps = depth // total.shape[1]

    def spread(value):
        value = jnp.broadcast_to(value, (ROWS, value.shape[1]))
        return jnp.concatenate([value] * reps, axis=1)

    along = [spread(value) for value in along]
    left = [spread(value) for value in left]
    copies = []
    for component in range(3):
        for plane in range(PLANES):
            spot = component * PLANES + plane
            images = [image_ref[k, spot] for k in range(ITERS + 1)]
            value = sum(a * b for a, b in zip(along, images[:ITERS]))
            solution_ref[component, plane] = value * inverse_ref[plane]
            residual_ref[component, plane] = sum(a * b for a, b in zip(left, images))
        for source, target in ((solution_ref, solution_out), (residual_ref, residual_out)):
            copies.append(
                pltpu.make_async_copy(
                    source.at[component], target.at[component], sent.at[len(copies)]
                )
            )
            copies[-1].start()
    for copy in copies:
        copy.wait()


def shaped(*shape):
    return jax.ShapeDtypeStruct(shape, jnp.float32)


def row_neighbours(low_part, high_part):
    count = lax.axis_size("cross")
    forward = [(i, i + 1) for i in range(count - 1)]
    backward = [(target, source) for source, target in forward]
    return lax.ppermute(high_part, "cross", forward), lax.ppermute(low_part, "cross", backward)


def next_chip(part):
    pairs = [(i, i + 1) for i in range(1, members(DIG) - 1, 2)]
    return lax.ppermute(part, DIG, pairs + [(target, source) for source, target in pairs])


def members(axes):
    return math.prod(lax.axis_size(name) for name in axes)


def exchanged(rows, axes):
    return lax.all_to_all(rows, axes, 0, 0, tiled=True)


def call(kernel, outs, *args, **options):
    return pl.pallas_call(
        kernel,
        out_shape=outs,
        compiler_params=pltpu.CompilerParams(vmem_limit_bytes=32 << 20),
        **options,
    )(*args)


def local(rhs_force, moduli, fixed_nodes, contact_nodes):
    depth = rhs_force.shape[3]
    count = (FIELDS + 1) * PLANES
    edge = shaped(count, EDGE, depth)
    arguments = (rhs_force, moduli, fixed_nodes, contact_nodes)
    arguments = [pltpu.with_memory_space_constraint(value, pltpu.HBM) for value in arguments]
    both, low, high = call(
        rows_kernel,
        (shaped(count, ROWS, depth), edge, edge),
        *arguments,
        in_specs=[pl.BlockSpec(memory_space=pltpu.HBM)] * len(arguments),
        scratch_shapes=[pltpu.VMEM(value.shape, value.dtype) for value in arguments]
        + [pltpu.SemaphoreType.DMA((len(arguments),))],
    )
    below, above = row_neighbours(low, high)
    tall, inside, outside = call(
        planes_kernel,
        (shaped(count, TALL, depth), shaped(2 * HALF, TALL, depth), shaped(HALF, TALL, depth)),
        both,
        below,
        above,
    )
    outside = next_chip(outside)
    inside = exchanged(inside, ("core",))
    image, inverse, moments = call(
        krylov_kernel,
        (
            shaped(ITERS + 1, 3 * PLANES, ROWS, depth),
            shaped(PLANES, ROWS, depth),
            shaped(members(SUM_FIRST), 128),
        ),
        tall,
        inside,
        outside,
    )
    moments = exchanged(moments, SUM_FIRST)
    moments = call(sum_kernel, shaped(members(SUM_LAST), 128), moments)
    moments = exchanged(moments, SUM_LAST)
    out = shaped(3, PLANES, ROWS, depth)
    return tuple(
        call(
            finish_kernel,
            (out, out),
            image,
            inverse,
            moments,
            out_specs=[pl.BlockSpec(memory_space=pltpu.HBM)] * 2,
            scratch_shapes=[pltpu.VMEM(out.shape, out.dtype)] * 2
            + [pltpu.SemaphoreType.DMA((6,))],
        )
    )


def solution(mesh):
    parts = DIG_SIZES + (mesh.shape["cross"],)
    split = jax.sharding.Mesh(mesh.devices.reshape(parts), DIG + ("cross",))
    return jax.shard_map(
        local,
        mesh=split,
        in_specs=(
            P(None, DIG, "cross", None),
            P(DIG, "cross", None),
            P(DIG, "cross", None),
            P(DIG, "cross", None),
        ),
        out_specs=(P(None, DIG, "cross", None), P(None, DIG, "cross", None)),
        check_vma=False,
    )
```
